32 devices in a mesh: row: 4 (over y, x), col: 8 (over z, core).
Axes of the slice: x: 2, y: 2, z: 4, core: 2. Of those that a mesh axis runs over, the one named last changes fastest.
Arguments:
- vectors: float32 [4608, 4096], P('row', 'col'), may hold values from -6 to 6
- reflectors: float32 [256, 2304], P('col', 'row'), may hold values from -0.75 to 0.75
Outputs:
- result: float32 [4608, 4096], P('row', 'col')
The draws below stay inside these ranges and needn't reach their ends.
All inputs are finite; a program needn't handle non-finite values.
Results may differ from the reference program's by a relative error of at most 0.00019.
Values sent between devices are 32-bit elements; how exact they have to be, the bound alone decides.
A program may use at most 64 MiB of HBM per device.

```python
import jax
import jax.numpy as jnp
from jax import lax

BAND = 64
GROUPS = 4
ROWS = 4608
COLS = 4096
REFLS = 256


def levels(own_key, extent, shards, smallest, high):
    level, own = 1.0, jax.random.fold_in(own_key, 6)
    for axis_at, parts in shards:
        heights = jnp.exp(jax.random.uniform(jax.random.fold_in(own, axis_at), (parts,), jnp.float32, smallest / len(shards), high / len(shards)))
        level = level * jnp.repeat(heights, extent[axis_at] // parts).reshape([-1 if axis == axis_at else 1 for axis in range(len(extent))])
    return level


def gaussian(own_key, shape, width, reach, shards=(), kind=jnp.bfloat16):
    array = width * jax.random.normal(own_key, shape, jnp.float32)
    if shards:
        array = array * levels(own_key, shape, shards, -0.22, 0.18)
    return jnp.clip(array, -reach, reach).astype(kind)


def setup_inputs(seed: int = 0) -> dict:
    key_of = jax.random.split(jax.random.key(seed), 3)
    vectors = gaussian(key_of[0], (ROWS, COLS), 1.0, 6.0, ((0, 4), (1, 8)), jnp.float32)
    reflectors = gaussian(key_of[1], (REFLS, ROWS // 2), BAND ** -0.5, 0.75, ((0, 8), (1, 4)), jnp.float32)
    return dict(vectors=vectors, reflectors=reflectors)


def upper_inverse(upper):
    diag_part = jnp.diagonal(upper, axis1=1, axis2=2)
    identity = jnp.eye(BAND, dtype=jnp.float32)
    nilpotent = upper / diag_part[:, :, None] - identity
    power = nilpotent
    inverse = identity - nilpotent
    for level in range(5):
        power = jnp.einsum("wab,wbc->wac", power, power, precision=lax.Precision.HIGHEST)
        inverse = jnp.einsum("wab,wbc->wac", inverse, identity + power, precision=lax.Precision.HIGHEST)
    return inverse / diag_part[:, None, :]


def reflector_blocks(compact):
    windows = compact.shape[0]
    column = lax.broadcasted_iota(jnp.int32, compact.shape, 2)
    filled = jnp.where(column == 0, jnp.float32(1.0), compact)
    padded = jnp.pad(filled, ((0, 0), (0, 0), (0, BAND + 1)))
    skewed = padded.reshape(windows, BAND * (2 * BAND + 1))[:, :2 * BAND * BAND].reshape(windows, BAND, 2 * BAND)
    gram_matrix = jnp.einsum("wji,wli->wjl", skewed, skewed, precision=lax.Precision.HIGHEST)
    upper_inv = jnp.triu(gram_matrix, 1) + 0.5 * gram_matrix * jnp.eye(BAND, dtype=jnp.float32)
    return skewed, upper_inverse(upper_inv)


def reflect_windows(blocks, skewed, inverse, weight):
    inner_prod = jnp.einsum("wji,wic->wjc", skewed, blocks, precision=lax.Precision.HIGHEST)
    solved = jnp.einsum("wjl,wlc->wjc", inverse, inner_prod, precision=lax.Precision.HIGHEST)
    change = jnp.einsum("wji,wjc->wic", skewed, solved, precision=lax.Precision.HIGHEST)
    return blocks - weight[:, None, None] * change


def reference(vectors, reflectors):
    all_rows = vectors.shape[0]
    result = vectors
    for group_index in range(GROUPS):
        offset = BAND * (group_index % 2)
        windows = (all_rows - offset) // (2 * BAND)
        compact = reflectors[group_index * BAND:(group_index + 1) * BAND, :windows * BAND]
        compact = compact.reshape(BAND, windows, BAND).transpose(1, 0, 2)
        skewed, inverse = reflector_blocks(compact)
        blocks = result[offset:offset + windows * 2 * BAND].reshape(windows, 2 * BAND, -1)
        blocks = reflect_windows(blocks, skewed, inverse, jnp.ones((windows,), jnp.float32))
        result = jnp.concatenate([result[:offset], blocks.reshape(windows * 2 * BAND, -1), result[offset + windows * 2 * BAND:]], 0)
    return result
```

```python
import functools

import jax
import jax.numpy as jnp
from jax import lax
from jax.experimental import pallas as pl
from jax.experimental.pallas import tpu as pltpu
from jax.sharding import PartitionSpec as P

BAND = 64
GROUPS = 4
WIN = 2 * BAND
HALO = 2 * BAND


def split(x):
    high = x.astype(jnp.bfloat16)
    low = (x - high.astype(jnp.float32)).astype(jnp.bfloat16)
    return high, low


def dot(a, b, dims=(1, 0)):
    return lax.dot_general(
        a, b, (((dims[0],), (dims[1],)), ((), ())), preferred_element_type=jnp.float32
    )


def product(a, b):
    ah, al = split(a)
    bh, bl = split(b)
    return dot(jnp.concatenate([ah, al], 1), jnp.concatenate([bh, bh], 0)) + dot(ah, bl)


def build_group(own, rows_axis, group, refl, q_ref):
    grid_row = lax.axis_index("row")
    size = WIN
    pairs = refl.shape[1] // size
    row = lax.broadcasted_iota(jnp.int32, (size, size), 0)
    lane = lax.broadcasted_iota(jnp.int32, (size, size), 1)
    eye = row == lane
    identity = eye.astype(jnp.float32)
    upper = (row // BAND == lane // BAND) & (row < lane)
    inside = (row // BAND) == (lane // BAND)
    lead = inside & (lane % BAND == 0)

    skews, nils, invs, scaled = [], [], [], []
    for pair in range(pairs):
        slab = refl[:, pair * size : (pair + 1) * size]
        both = jnp.concatenate([slab, slab], 0)
        both = jnp.where(lead, 1.0, jnp.where(inside, both, 0.0))
        skews.append(pltpu.roll(both, 0, 1, stride=1, stride_axis=0))
    for pair in range(pairs):
        high, low = split(skews[pair])
        gram = dot(
            jnp.concatenate([high, low], 1), jnp.concatenate([high, high], 1), (1, 1)
        ) + dot(high, low, (1, 1))
        diag = 0.5 * jnp.sum(jnp.where(eye, gram, 0.0), axis=1, keepdims=True)
        scale = 1.0 / diag
        nils.append(jnp.where(upper, gram * scale, 0.0))
        scaled.append(skews[pair] * scale)
    block = BAND // 4
    near = row // block == lane // block
    powers = [jnp.where(near, n, 0.0) for n in nils]
    invs = [identity - p for p in powers]
    powers = [product(p, p) for p in powers]
    for level in range(2):
        stacked = [product(jnp.concatenate([i, p], 0), p) for i, p in zip(invs, powers)]
        invs = [i + s[:size] for i, s in zip(invs, stacked)]
        powers = [s[size:] for s in stacked]
    invs = [i + product(i, p) for i, p in zip(invs, powers)]
    for _ in range(2):
        wide = row // (2 * block) == lane // (2 * block)
        far = wide & (row // block != lane // block)
        cross = [product(jnp.where(far, n, 0.0), i) for n, i in zip(nils, invs)]
        invs = [i - product(i, c) for i, c in zip(invs, cross)]
        block *= 2
    solved = [product(i, s) for i, s in zip(invs, scaled)]
    usable = own * rows_axis - group % 2
    outer = jnp.where(group == 2, grid_row < rows_axis - 1, grid_row > 0)
    for pair in range(pairs):
        sh, sl = split(skews[pair])
        th, tl = split(solved[pair])
        for half in range(2):
            k = 2 * pair + half
            at = slice(half * BAND, (half + 1) * BAND)
            left = jnp.concatenate([sh[at], sl[at], sh[at]], 0)
            right = jnp.concatenate([th[at], th[at], tl[at]], 0)
            change = dot(left, right, (0, 0))
            valid = outer if k == own else grid_row * own + k < usable
            high, low = split(identity - jnp.where(valid, change, 0.0))
            q_ref[group, k, :, :size] = high
            q_ref[group, k, :, size:] = low


def mixed(a, b, count):
    total, bit = 0, 1
    while bit < count:
        total = total + ((a // bit + b // bit) % 2) * bit
        bit *= 2
    return total


def turn(q, x):
    xh, xl = split(x)
    return dot(q, jnp.concatenate([xh, xh], 0)) + dot(q[:, :WIN], xl)


def over_tiles(columns, step):
    tile = min(columns, 256)

    def one_tile(i, carry):
        step(pl.ds(pl.multiple_of(i * tile, tile), tile))
        return carry

    lax.fori_loop(0, columns // tile, one_tile, 0)


def apply_windows(windows, q_ref, work):
    def step(cols):
        for group, k, at, low, high in windows:
            y = turn(q_ref[group, k, low:high], work[at : at + WIN, cols])
            work[at + low : at + high, cols] = y

    over_tiles(work.shape[1], step)


def back_kernel(
    own, rows_axis, cols_axis, refl_ref, x_ref, out_ref,
    q_ref, work, raw, edge, beside, slab, ex,
    near_send, near_recv, line_send, line_recv, pair_send, pair_recv, ex_send, ex_recv, own_sem, x_sem, out_sem,
):
    row, me = lax.axis_index("row"), lax.axis_index("col")
    chips = cols_axis // 2
    chip, core = me // 2, me % 2
    up, down = (row + rows_axis - 1) % rows_axis, (row + 1) % rows_axis
    other = chip * 2 + 1 - core
    rows, columns = x_ref.shape
    stored = raw.shape[1]
    last = stored - BAND
    share_group = cols_axis // GROUPS
    group_of = me // share_group
    two = 2 * share_group
    has_up, has_down = row > 0, row < rows_axis - 1
    mesh_ids = pl.DeviceIdType.MESH

    def remote(source, target, send, recv, device):
        return pltpu.make_async_remote_copy(
            src_ref=source, dst_ref=target, send_sem=send, recv_sem=recv,
            device_id=device, device_id_type=mesh_ids,
        )

    local = pltpu.make_async_copy(refl_ref, raw, own_sem)
    local.start()
    fill = pltpu.make_async_copy(x_ref, work.at[pl.ds(HALO, rows)], x_sem)
    fill.start()
    first, third = group_of == 0, group_of == 2
    barrier = pltpu.get_barrier_semaphore()
    partners = [(row, mixed(chip, i, chips) * 2 + core) for i in range(1, chips)]
    partners += [(row, other), (up, me), (down, me)]

    def greet(partner):
        pl.semaphore_signal(barrier, inc=1, device_id=partner, device_id_type=mesh_ids)

    for partner in partners:
        greet(partner)
    pl.when(first)(lambda: greet((up, (me + two) % cols_axis)))
    pl.when(third)(lambda: greet((down, (me + cols_axis - two) % cols_axis)))

    @pl.when(jnp.logical_not(has_up))
    def _():
        work[0:HALO] = jnp.zeros((HALO, columns), jnp.float32)
        ex[0] = jnp.zeros((BAND, columns), jnp.float32)

    @pl.when(jnp.logical_not(has_down))
    def _():
        work[HALO + rows :] = jnp.zeros((HALO, columns), jnp.float32)
        ex[1] = jnp.zeros((BAND, columns), jnp.float32)

    gets_near = jnp.where(third, has_down, has_up)

    @pl.when(jnp.logical_not(gets_near))
    def _():
        beside[...] = jnp.zeros(beside.shape, jnp.float32)

    local.wait()
    edge[:, :BAND] = raw[:, last:]
    edge[:, BAND:] = jnp.zeros((raw.shape[0], BAND), jnp.float32)
    slab[me, :, :stored] = raw[...]
    pl.semaphore_wait(barrier, len(partners) + jnp.where(first | third, 1, 0))

    tail = remote(edge, beside, near_send.at[0], near_recv.at[0], (down, me))
    head = remote(slab.at[me, :, pl.ds(0, WIN)], beside, near_send.at[1], near_recv.at[0], (up, (me + two) % cols_axis))
    sends_tail = has_down & jnp.logical_not(third)
    sends_head = has_up & first
    pl.when(sends_tail)(tail.start)
    pl.when(sends_head)(head.start)
    pending = []

    def share(kind):
        cols = pl.ds(0, last) if kind == 0 else pl.ds(last, WIN)
        mine = slab.at[me, :, cols]
        pair = remote(mine, mine, pair_send.at[kind, chip], pair_recv.at[kind, chip], (row, other))
        pair.start()
        pending.append(pair)
        for i in range(1, chips):
            there = mixed(chip, i, chips)
            line = remote(mine, mine, line_send.at[kind, there], line_recv.at[kind, chip], (row, there * 2 + core))
            line.start()
            pending.append(line)

    share(0)
    above = remote(
        x_ref.at[pl.ds(rows - HALO, HALO)], work.at[pl.ds(0, HALO)], ex_send.at[0], ex_recv.at[0], (down, me)
    )
    below = remote(
        x_ref.at[pl.ds(0, HALO)], work.at[pl.ds(HALO + rows, HALO)], ex_send.at[1], ex_recv.at[1], (up, me)
    )
    pl.when(has_down)(above.start)
    pl.when(has_up)(below.start)
    pl.when(gets_near)(tail.wait_recv)
    slab[me, :, last:] = jnp.where(
        lax.broadcasted_iota(jnp.int32, edge.shape, 1) < BAND, edge[...], pltpu.roll(beside[...], BAND, 1)
    )
    share(1)

    def arrived(kind, there, mine, recv):
        cols = pl.ds(0, last) if kind == 0 else pl.ds(last, WIN)
        slot = slab.at[there * 2 + (core if mine else 1 - core), :, cols]
        remote(slot, slot, own_sem, recv.at[kind, there], (row, other)).wait_recv()

    chip_group = share_group // 2
    mine = chip // chip_group

    def members(i):
        base = mixed(mine, i, GROUPS) * chip_group
        return [base + mixed(chip % chip_group, j, chip_group) for j in range(chip_group)]

    def forward(i):
        for j, there in enumerate(members(i)):
            if i == 0 and j == 0:
                continue
            for kind in range(2):
                arrived(kind, there, True, line_recv)
                cols = pl.ds(0, last) if kind == 0 else pl.ds(last, WIN)
                slot = slab.at[there * 2 + core, :, cols]
                copy = remote(slot, slot, pair_send.at[kind, there], pair_recv.at[kind, there], (row, other))
                copy.start()
                pending.append(copy)

    def build(i):
        for there in members(i):
            for kind in range(2):
                arrived(kind, there, False, pair_recv)
        group = mixed(mine, i, GROUPS)
        refl = slab[pl.ds(group * share_group, share_group)].reshape(BAND, slab.shape[2])
        build_group(own, rows_axis, group, refl, q_ref)

    forward(0)
    build(0)
    forward(1)
    for i in range(1, GROUPS):
        if i + 1 < GROUPS:
            forward(i + 1)
        build(i)

    def window(group, k):
        return group, k, HALO + BAND * (group % 2) + WIN * k, 0, WIN

    edges = [
        (0, own, 0, BAND, WIN),
        window(0, 0),
        window(0, 1),
        window(0, own - 2),
        window(0, own - 1),
        (2, own, HALO + rows, 0, BAND),
        (1, own, HALO - BAND, BAND, WIN),
        window(1, 0),
        window(1, own - 2),
        (1, own - 1, HALO + rows - BAND, 0, BAND),
        window(2, 0),
        window(2, own - 1),
    ]
    inner = [window(0, k) for k in range(2, own - 2)]
    inner += [window(1, k) for k in range(1, own - 2)]
    inner += [window(2, k) for k in range(1, own - 1)]
    inner += [window(3, k) for k in range(own - 1)]

    fill.wait()
    pl.when(has_up)(above.wait_recv)
    pl.when(has_down)(below.wait_recv)
    apply_windows(edges, q_ref, work)
    to_up = remote(work.at[pl.ds(HALO, BAND)], ex.at[1], ex_send.at[2], ex_recv.at[2], (up, me))
    to_down = remote(work.at[pl.ds(HALO + rows - BAND, BAND)], ex.at[0], ex_send.at[3], ex_recv.at[3], (down, me))
    pl.when(has_up)(to_up.start)
    pl.when(has_down)(to_down.start)
    apply_windows(inner, q_ref, work)

    def result(start, size, at):
        return pltpu.make_async_copy(
            work.at[pl.ds(HALO + start, size)], out_ref.at[pl.ds(start, size)], out_sem.at[at]
        )

    results = [result(BAND, rows - 2 * BAND, 0), result(0, BAND, 1), result(rows - BAND, BAND, 2)]
    results[0].start()
    pl.when(has_up)(to_up.wait_send)
    pl.when(has_down)(to_down.wait_send)
    pl.when(has_down)(to_up.wait_recv)
    pl.when(has_up)(to_down.wait_recv)

    def straddle(cols):
        top = slice(HALO, HALO + BAND)
        bottom = slice(HALO + rows - BAND, HALO + rows)
        x = jnp.concatenate([ex[0, :, cols], work[top, cols]], 0)
        work[top, cols] = turn(q_ref[3, own, BAND:], x)
        x = jnp.concatenate([work[bottom, cols], ex[1, :, cols]], 0)
        work[bottom, cols] = turn(q_ref[3, own - 1, :BAND], x)

    over_tiles(columns, straddle)
    results[1].start()
    results[2].start()
    pl.when(sends_tail)(tail.wait_send)
    pl.when(sends_head)(head.wait_send)
    pl.when(has_down)(above.wait_send)
    pl.when(has_up)(below.wait_send)
    for copy in pending:
        copy.wait_send()
    for copy in results:
        copy.wait()


def shards(vectors, reflectors):
    rows, columns = vectors.shape
    own = rows // WIN
    rows_axis, cols_axis = lax.axis_size("row"), lax.axis_size("col")
    slots, stored = reflectors.shape
    chips = cols_axis // 2
    dma = pltpu.SemaphoreType.DMA
    return pl.pallas_call(
        functools.partial(back_kernel, own, rows_axis, cols_axis),
        in_specs=[pl.BlockSpec(memory_space=pltpu.HBM)] * 2,
        out_specs=pl.BlockSpec(memory_space=pl.ANY),
        out_shape=jax.ShapeDtypeStruct(vectors.shape, vectors.dtype),
        scratch_shapes=[
            pltpu.VMEM((GROUPS, own + 1, WIN, 2 * WIN), jnp.bfloat16),
            pltpu.VMEM((rows + 2 * HALO, columns), jnp.float32),
            pltpu.VMEM((slots, stored), jnp.float32),
            pltpu.VMEM((slots, WIN), jnp.float32),
            pltpu.VMEM((slots, WIN), jnp.float32),
            pltpu.VMEM((cols_axis, slots, stored + BAND), jnp.float32),
            pltpu.VMEM((2, BAND, columns), jnp.float32),
            dma((2,)),
            dma((1,)),
            dma((2, chips)),
            dma((2, chips)),
            dma((2, chips)),
            dma((2, chips)),
            dma((4,)),
            dma((4,)),
            dma,
            dma,
            dma((3,)),
        ],
        compiler_params=pltpu.CompilerParams(collective_id=0, has_side_effects=True, vmem_limit_bytes=50 * 2**20),
        name="back",
    )(reflectors, vectors)


def solution(mesh):
    placed = (P("row", "col"), P("col", "row"))
    return jax.shard_map(
        shards, mesh=mesh, in_specs=placed, out_specs=P("row", "col"), check_vma=False
    )
```

```python
import functools

import jax
import jax.numpy as jnp
from jax import lax
from jax.experimental import pallas as pl
from jax.experimental.pallas import tpu as pltpu
from jax.sharding import PartitionSpec as P

BAND = 64
GROUPS = 4
WIN = 2 * BAND
HALO = 2 * BAND


def split(x):
    high = x.astype(jnp.bfloat16)
    low = (x - high.astype(jnp.float32)).astype(jnp.bfloat16)
    return high, low


def dot(a, b, dims=(1, 0)):
    return lax.dot_general(
        a, b, (((dims[0],), (dims[1],)), ((), ())), preferred_element_type=jnp.float32
    )


def product(a, b):
    ah, al = split(a)
    bh, bl = split(b)
    return dot(jnp.concatenate([ah, al], 1), jnp.concatenate([bh, bh], 0)) + dot(ah, bl)


def keep(q, q_ref, group, k):
    high, low = split(q)
    q_ref[group, k, :, :WIN] = high
    q_ref[group, k, :, WIN:] = low


def build_windows(own, rows_axis, picks, q_ref, made=None):
    grid_row = lax.axis_index("row")
    size = WIN
    row = lax.broadcasted_iota(jnp.int32, (size, size), 0)
    lane = lax.broadcasted_iota(jnp.int32, (size, size), 1)
    eye = row == lane
    identity = eye.astype(jnp.float32)
    upper = (row // BAND == lane // BAND) & (row < lane)
    inside = (row // BAND) == (lane // BAND)
    lead = inside & (lane % BAND == 0)

    skews, nils, invs, scaled = [], [], [], []
    for (left, right), _ in picks:
        both = jnp.concatenate([left, right], 0)
        both = jnp.where(lead, 1.0, jnp.where(inside, both, 0.0))
        skews.append(pltpu.roll(both, 0, 1, stride=1, stride_axis=0))
    for skew in skews:
        high, low = split(skew)
        gram = dot(
            jnp.concatenate([high, low], 1), jnp.concatenate([high, high], 1), (1, 1)
        ) + dot(high, low, (1, 1))
        diag = 0.5 * jnp.sum(jnp.where(eye, gram, 0.0), axis=1, keepdims=True)
        scale = 1.0 / diag
        nils.append(jnp.where(upper, gram * scale, 0.0))
        scaled.append(skew * scale)
    block = BAND // 4
    near = row // block == lane // block
    powers = [jnp.where(near, n, 0.0) for n in nils]
    invs = [identity - p for p in powers]
    powers = [product(p, p) for p in powers]
    for level in range(2):
        stacked = [product(jnp.concatenate([i, p], 0), p) for i, p in zip(invs, powers)]
        invs = [i + s[:size] for i, s in zip(invs, stacked)]
        powers = [s[size:] for s in stacked]
    invs = [i + product(i, p) for i, p in zip(invs, powers)]
    for _ in range(2):
        wide = row // (2 * block) == lane // (2 * block)
        far = wide & (row // block != lane // block)
        cross = [product(jnp.where(far, n, 0.0), i) for n, i in zip(nils, invs)]
        invs = [i - product(i, c) for i, c in zip(invs, cross)]
        block *= 2
    solved = [product(i, s) for i, s in zip(invs, scaled)]
    for at, ((_, slots), skew, wing) in enumerate(zip(picks, skews, solved)):
        sh, sl = split(skew)
        th, tl = split(wing)
        for half, (group, k) in enumerate(slots):
            own_rows = slice(half * BAND, (half + 1) * BAND)
            left = jnp.concatenate([sh[own_rows], sl[own_rows], sh[own_rows]], 0)
            right = jnp.concatenate([th[own_rows], th[own_rows], tl[own_rows]], 0)
            change = dot(left, right, (0, 0))
            outer = jnp.where(group == 2, grid_row < rows_axis - 1, grid_row > 0)
            inner = grid_row * own + k < own * rows_axis - group % 2
            q = identity - jnp.where(jnp.where(k == own, outer, inner), change, 0.0)
            keep(q, q_ref, group, k)
            if made is not None and at < made.shape[0]:
                made[at, half] = q


def mixed(a, b, count):
    total, bit = 0, 1
    while bit < count:
        total = total + ((a // bit + b // bit) % 2) * bit
        bit *= 2
    return total


def turn(q, x):
    xh, xl = split(x)
    return dot(q, jnp.concatenate([xh, xh], 0)) + dot(q[:, :WIN], xl)


def over_tiles(columns, step):
    tile = min(columns, 256)

    def one_tile(i, carry):
        step(pl.ds(pl.multiple_of(i * tile, tile), tile))
        return carry

    lax.fori_loop(0, columns // tile, one_tile, 0)


def apply_windows(windows, q_ref, work):
    def step(cols):
        for group, k, at, low, high in windows:
            y = turn(q_ref[group, k, low:high], work[at : at + WIN, cols])
            work[at + low : at + high, cols] = y

    over_tiles(work.shape[1], step)


def tile_order(own):
    tiles = (own + 1) // 2
    return [0, tiles - 2] + list(range(1, tiles - 2)) + [tiles - 1]


def edge_pairs(own):
    last, third = own // 2, own // 2 - 1
    return [
        ((0, 0), (0, 0)),
        ((0, last), (0, last)),
        ((2, last), (0, third)),
        ((1, 0), (1, third)),
        ((1, last), (1, last)),
        ((2, 0), (2, last)),
    ]


def back_kernel(
    own, rows_axis, cols_axis, refl_ref, x_ref, out_ref,
    q_ref, work, raw, edge, beside, slab, ex, relayed, late, made, given,
    near_send, near_recv, line_send, line_recv, pair_send, pair_recv, halo_send, halo_recv, swap_send, swap_recv, own_sem, x_sem,
):
    row, me = lax.axis_index("row"), lax.axis_index("col")
    chips = cols_axis // 2
    chip, core = me // 2, me % 2
    up, down = (row + rows_axis - 1) % rows_axis, (row + 1) % rows_axis
    other = chip * 2 + 1 - core
    rows, columns = x_ref.shape
    stored = raw.shape[1]
    order = tile_order(own)
    share_group = cols_axis // GROUPS
    group_of = me // share_group
    two = 2 * share_group
    has_up, has_down = row > 0, row < rows_axis - 1
    mesh_ids = pl.DeviceIdType.MESH
    no = jnp.logical_not
    detour = rows_axis == 4
    across = (row + 2) % rows_axis

    def remote(source, target, send, recv, device):
        return pltpu.make_async_remote_copy(
            src_ref=source, dst_ref=target, send_sem=send, recv_sem=recv,
            device_id=device, device_id_type=mesh_ids,
        )

    local = pltpu.make_async_copy(refl_ref, raw, own_sem)
    local.start()
    fill = pltpu.make_async_copy(x_ref, work.at[pl.ds(HALO, rows)], x_sem)
    fill.start()
    first, third = group_of == 0, group_of == 2
    barrier = pltpu.get_barrier_semaphore()
    partners = [(row, mixed(chip, i, chips) * 2 + core) for i in range(1, chips)]
    partners += [(row, other), (up, me), (down, me)]
    if detour:
        partners.append((across, me))

    def greet(partner):
        pl.semaphore_signal(barrier, inc=1, device_id=partner, device_id_type=mesh_ids)

    for partner in partners:
        greet(partner)
    pl.when(first)(lambda: greet((up, (me + two) % cols_axis)))
    pl.when(third)(lambda: greet((down, (me + cols_axis - two) % cols_axis)))

    @pl.when(no(has_up))
    def _():
        work[0:HALO] = jnp.zeros((HALO, columns), jnp.float32)
        ex[0] = jnp.zeros((BAND, columns), jnp.float32)

    @pl.when(no(has_down))
    def _():
        work[HALO + rows :] = jnp.zeros((HALO, columns), jnp.float32)
        ex[1] = jnp.zeros((BAND, columns), jnp.float32)

    gets_near = jnp.where(third, has_down, has_up)

    @pl.when(no(gets_near))
    def _():
        beside[...] = jnp.zeros(beside.shape, jnp.float32)

    local.wait()
    edge[:, :BAND] = raw[:, stored - BAND :]
    edge[:, BAND:] = jnp.zeros((raw.shape[0], BAND), jnp.float32)
    for at, tile in enumerate(order[:-1]):
        slab[me, :, at * WIN : (at + 1) * WIN] = raw[:, tile * WIN : (tile + 1) * WIN]
    pl.semaphore_wait(barrier, len(partners) + jnp.where(first | third, 1, 0))

    last = (len(order) - 1) * WIN
    spans = (pl.ds(0, 2 * WIN), pl.ds(last, WIN), pl.ds(2 * WIN, last - 2 * WIN))
    tail = remote(edge, beside, near_send.at[0], near_recv.at[0], (down, me))
    head = remote(slab.at[me, :, pl.ds(0, WIN)], beside, near_send.at[1], near_recv.at[0], (up, (me + two) % cols_axis))
    sends_tail = has_down & no(third)
    sends_head = has_up & first
    pl.when(sends_tail)(tail.start)
    pl.when(sends_head)(head.start)
    pending = []

    def share_pair(kind):
        part = slab.at[me, :, spans[kind]]
        pair = remote(part, part, pair_send.at[kind, chip], pair_recv.at[kind, chip], (row, other))
        pair.start()
        pending.append(pair)

    def share_line(kind):
        part = slab.at[me, :, spans[kind]]
        for i in range(1, chips):
            there = mixed(chip, i, chips)
            line = remote(part, part, line_send.at[kind, there], line_recv.at[kind, chip], (row, there * 2 + core))
            line.start()
            pending.append(line)

    def exchange(at, down_from, up_from, top, bottom, held):
        half = columns // 2
        left, right = pl.ds(0, half), pl.ds(half, half)
        send, recv = halo_send.at[at], halo_recv.at[at]

        def flow(index, source, target, cols, device):
            return remote(source.at[:, cols], target.at[:, cols], send.at[index], recv.at[index], device)

        above = [flow(0, down_from, top, left, (down, me)), flow(1, down_from, top, right, (down, me))]
        below = [flow(2, up_from, bottom, left, (up, me)), flow(3, up_from, bottom, right, (up, me))]
        starts = []
        relays = []
        if detour:
            starts.append((row == 1, remote(down_from.at[:, right], held, send.at[1], recv.at[4], (across, me))))
            starts.append((row == 2, remote(up_from.at[:, right], held, send.at[3], recv.at[4], (across, me))))
            relays.append((row == 3, remote(held, top.at[:, right], send.at[4], recv.at[1], (up, me))))
            relays.append((row == 0, remote(held, bottom.at[:, right], send.at[4], recv.at[3], (down, me))))
        starts += [(has_down, above[0]), (has_up, below[0])]
        starts.append((has_down & (row != 1) if detour else has_down, above[1]))
        starts.append((has_up & (row != 2) if detour else has_up, below[1]))

        def start():
            for here, copy in starts:
                pl.when(here)(copy.start)

        def relay():
            for here, copy in relays:
                arrival = remote(held, held, send.at[4], recv.at[4], (across, me))

                @pl.when(here)
                def _():
                    arrival.wait_recv()
                    copy.start()

        def wait_recv():
            for copy in above:
                pl.when(has_up)(copy.wait_recv)
            for copy in below:
                pl.when(has_down)(copy.wait_recv)

        def wait_send():
            for here, copy in starts + relays:
                pl.when(here)(copy.wait_send)

        return start, relay, wait_recv, wait_send

    early = exchange(
        0, x_ref.at[pl.ds(rows - HALO, HALO)], x_ref.at[pl.ds(0, HALO)],
        work.at[pl.ds(0, HALO)], work.at[pl.ds(HALO + rows, HALO)], relayed,
    )
    final = exchange(
        1, work.at[pl.ds(HALO + rows - BAND, BAND)], work.at[pl.ds(HALO, BAND)], ex.at[0], ex.at[1], late,
    )

    share_pair(0)
    share_pair(2)
    share_line(0)
    early[0]()
    pl.when(gets_near)(tail.wait_recv)
    slab[me, :, last:] = jnp.where(
        lax.broadcasted_iota(jnp.int32, edge.shape, 1) < BAND, edge[...], pltpu.roll(beside[...], BAND, 1)
    )
    share_pair(1)
    share_line(1)

    def forward(kind):
        for i in range(1, chips):
            there = mixed(chip, i, chips)
            slot = slab.at[there * 2 + core, :, spans[kind]]
            copy = remote(slot, slot, pair_send.at[kind, there], pair_recv.at[kind, there], (row, other))
            remote(slot, slot, own_sem, line_recv.at[kind, there], (row, other)).wait_recv()
            copy.start()
            pending.append(copy)

    def landed(kind, there):
        slot = slab.at[there * 2 + 1 - core, :, spans[kind]]
        remote(slot, slot, own_sem, pair_recv.at[kind, there], (row, other)).wait_recv()

    chip_group = share_group // 2
    mine = chip // chip_group

    def taken(group, at):
        part = slab[pl.ds(group * share_group, share_group), :, pl.ds(at, WIN)]
        return part.reshape(BAND, WIN)

    def build(pairs):
        picks = []
        for sides in pairs:
            parts = [taken(group, order.index(tile) * WIN) for group, tile in sides]
            slots = [(group, 2 * tile + half) for half, (group, tile) in enumerate(sides)]
            picks.append((parts, slots))
        build_windows(own, rows_axis, picks, q_ref)

    tiles = len(order)
    others = [mixed(mine, i, GROUPS) for i in range(1, GROUPS)]
    turns = [(group, tile) for tile in range((tiles - 1) // 2) for group in others]

    def build_half():
        picks = []
        for group, tile in turns:
            far = tile + (tiles - 1) // 2
            at = jnp.where(core == 0, order.index(tile) * WIN, order.index(far) * WIN)
            part = taken(group, pl.multiple_of(at, WIN))
            k = 2 * jnp.where(core == 0, tile, far)
            picks.append(((part, part), [(group, k), (group, k + 1)]))
        part = taken(3, (tiles - 1) * WIN)
        picks.append(((part, part), [(3, own - 1), (3, own)]))
        build_windows(own, rows_axis, picks, q_ref, made)
        for at in range(len(turns)):
            swaps[at].start()

    def take_half():
        for at, (group, tile) in enumerate(turns):
            swaps[at].wait_recv()
            k = 2 * jnp.where(core == 1, tile, tile + (tiles - 1) // 2)
            for half in range(2):
                keep(given[at, half], q_ref, group, k + half)

    swaps = [
        remote(made.at[at], given.at[at], swap_send.at[at], swap_recv.at[at], (row, other))
        for at in range(len(turns))
    ]
    whole_group = [((mine, tile),) * 2 for tile in range(tiles)]
    for kind in (0, 2, 1):
        landed(kind, chip)
    if chip_group == 1:
        build(whole_group)
    share_line(2)
    early[1]()
    for kind in range(2):
        forward(kind)
    for kind in range(2):
        for i in range(1, chips):
            landed(kind, mixed(chip, i, chips))
    build(edge_pairs(own))

    def window(group, k):
        return group, k, HALO + BAND * (group % 2) + WIN * k, 0, WIN

    edges = [
        (0, own, 0, BAND, WIN),
        window(0, 0),
        window(0, 1),
        window(0, own - 2),
        window(0, own - 1),
        (2, own, HALO + rows, 0, BAND),
        (1, own, HALO - BAND, BAND, WIN),
        window(1, 0),
        window(1, own - 2),
        (1, own - 1, HALO + rows - BAND, 0, BAND),
        window(2, 0),
        window(2, own - 1),
    ]
    inner = [window(0, k) for k in range(2, own - 2)]
    inner += [window(1, k) for k in range(1, own - 2)]
    inner += [window(2, k) for k in range(1, own - 1)]

    fill.wait()
    forward(2)
    early[2]()
    apply_windows(edges, q_ref, work)
    final[0]()
    for i in range(1, chips):
        landed(2, mixed(chip, i, chips))
    if chip_group > 1:
        build(whole_group)
    build_half()
    final[1]()
    take_half()
    apply_windows(inner, q_ref, work)

    def finish(cols):
        for k in range(own - 1):
            at = BAND + WIN * k
            out_ref[at : at + WIN, cols] = turn(q_ref[3, k], work[HALO + at : HALO + at + WIN, cols])

    over_tiles(columns, finish)
    final[2]()

    def straddle(cols):
        x = jnp.concatenate([ex[0, :, cols], work[HALO : HALO + BAND, cols]], 0)
        out_ref[:BAND, cols] = turn(q_ref[3, own, BAND:], x)
        x = jnp.concatenate([work[HALO + rows - BAND : HALO + rows, cols], ex[1, :, cols]], 0)
        out_ref[rows - BAND :, cols] = turn(q_ref[3, own - 1, :BAND], x)

    over_tiles(columns, straddle)
    pl.when(sends_tail)(tail.wait_send)
    pl.when(sends_head)(head.wait_send)
    early[3]()
    final[3]()
    for copy in pending + swaps:
        copy.wait_send()


def shards(vectors, reflectors):
    rows, columns = vectors.shape
    own = rows // WIN
    rows_axis, cols_axis = lax.axis_size("row"), lax.axis_size("col")
    slots, stored = reflectors.shape
    chips = cols_axis // 2
    turns = (GROUPS - 1) * (own // 4)
    dma = pltpu.SemaphoreType.DMA
    return pl.pallas_call(
        functools.partial(back_kernel, own, rows_axis, cols_axis),
        in_specs=[pl.BlockSpec(memory_space=pltpu.HBM)] * 2,
        out_specs=pl.BlockSpec(memory_space=pltpu.VMEM),
        out_shape=jax.ShapeDtypeStruct(vectors.shape, vectors.dtype),
        scratch_shapes=[
            pltpu.VMEM((GROUPS, own + 1, WIN, 2 * WIN), jnp.bfloat16),
            pltpu.VMEM((rows + 2 * HALO, columns), jnp.float32),
            pltpu.VMEM((slots, stored), jnp.float32),
            pltpu.VMEM((slots, WIN), jnp.float32),
            pltpu.VMEM((slots, WIN), jnp.float32),
            pltpu.VMEM((cols_axis, slots, stored + BAND), jnp.float32),
            pltpu.VMEM((2, BAND, columns), jnp.float32),
            pltpu.VMEM((HALO, columns // 2), jnp.float32),
            pltpu.VMEM((BAND, columns // 2), jnp.float32),
            pltpu.VMEM((turns, 2, WIN, WIN), jnp.float32),
            pltpu.VMEM((turns, 2, WIN, WIN), jnp.float32),
            dma((2,)),
            dma((1,)),
            dma((3, chips)),
            dma((3, chips)),
            dma((3, chips)),
            dma((3, chips)),
            dma((2, 5)),
            dma((2, 5)),
            dma((turns,)),
            dma((turns,)),
            dma,
            dma,
        ],
        compiler_params=pltpu.CompilerParams(collective_id=0, has_side_effects=True, vmem_limit_bytes=50 * 2**20),
        name="back",
    )(reflectors, vectors)


def solution(mesh):
    placed = (P("row", "col"), P("col", "row"))
    return jax.shard_map(
        shards, mesh=mesh, in_specs=placed, out_specs=P("row", "col"), check_vma=False
    )
```

```python
import functools

import jax
import jax.numpy as jnp
from jax import lax
from jax.experimental import pallas as pl
from jax.experimental.pallas import tpu as pltpu
from jax.sharding import PartitionSpec as P

BAND = 64
GROUPS = 4
WIN = 2 * BAND
HALO = 2 * BAND


def split(x):
    high = x.astype(jnp.bfloat16)
    low = (x - high.astype(jnp.float32)).astype(jnp.bfloat16)
    return high, low


def dot(a, b, dims=(1, 0)):
    return lax.dot_general(
        a, b, (((dims[0],), (dims[1],)), ((), ())), preferred_element_type=jnp.float32
    )


def product(a, b):
    ah, al = split(a)
    bh, bl = split(b)
    return dot(jnp.concatenate([ah, al], 1), jnp.concatenate([bh, bh], 0)) + dot(ah, bl)


def keep(q, q_ref, group, k):
    high, low = split(q)
    q_ref[group, k, :, :WIN] = high
    q_ref[group, k, :, WIN:] = low


def build_windows(own, rows_axis, picks, q_ref):
    grid_row = lax.axis_index("row")
    size = WIN
    row = lax.broadcasted_iota(jnp.int32, (size, size), 0)
    lane = lax.broadcasted_iota(jnp.int32, (size, size), 1)
    eye = row == lane
    identity = eye.astype(jnp.float32)
    upper = (row // BAND == lane // BAND) & (row < lane)
    inside = (row // BAND) == (lane // BAND)
    lead = inside & (lane % BAND == 0)

    skews, nils, invs, scaled = [], [], [], []
    for (left, right), _ in picks:
        both = jnp.concatenate([left, right], 0)
        both = jnp.where(lead, 1.0, jnp.where(inside, both, 0.0))
        skews.append(pltpu.roll(both, 0, 1, stride=1, stride_axis=0))
    for skew in skews:
        high, low = split(skew)
        gram = dot(
            jnp.concatenate([high, low], 1), jnp.concatenate([high, high], 1), (1, 1)
        ) + dot(high, low, (1, 1))
        diag = 0.5 * jnp.sum(jnp.where(eye, gram, 0.0), axis=1, keepdims=True)
        scale = 1.0 / diag
        nils.append(jnp.where(upper, gram * scale, 0.0))
        scaled.append(skew * scale)
    block = BAND // 4
    near = row // block == lane // block
    powers = [jnp.where(near, n, 0.0) for n in nils]
    invs = [identity - p for p in powers]
    powers = [product(p, p) for p in powers]
    for level in range(2):
        stacked = [product(jnp.concatenate([i, p], 0), p) for i, p in zip(invs, powers)]
        invs = [i + s[:size] for i, s in zip(invs, stacked)]
        powers = [s[size:] for s in stacked]
    invs = [i + product(i, p) for i, p in zip(invs, powers)]
    for _ in range(2):
        wide = row // (2 * block) == lane // (2 * block)
        far = wide & (row // block != lane // block)
        cross = [product(jnp.where(far, n, 0.0), i) for n, i in zip(nils, invs)]
        invs = [i - product(i, c) for i, c in zip(invs, cross)]
        block *= 2
    solved = [product(i, s) for i, s in zip(invs, scaled)]
    for (_, slots), skew, wing in zip(picks, skews, solved):
        sh, sl = split(skew)
        th, tl = split(wing)
        for half, (group, k) in enumerate(slots):
            own_rows = slice(half * BAND, (half + 1) * BAND)
            left = jnp.concatenate([sh[own_rows], sl[own_rows], sh[own_rows]], 0)
            right = jnp.concatenate([th[own_rows], th[own_rows], tl[own_rows]], 0)
            change = dot(left, right, (0, 0))
            outer = jnp.where(group == 2, grid_row < rows_axis - 1, grid_row > 0)
            inner = grid_row * own + k < own * rows_axis - group % 2
            q = identity - jnp.where(jnp.where(k == own, outer, inner), change, 0.0)
            keep(q, q_ref, group, k)


def mixed(a, b, count):
    total, bit = 0, 1
    while bit < count:
        total = total + ((a // bit + b // bit) % 2) * bit
        bit *= 2
    return total


def turn(q, x):
    xh, xl = split(x)
    return dot(q, jnp.concatenate([xh, xh], 0)) + dot(q[:, :WIN], xl)


def apply_windows(windows, q_ref, work, cols):
    for group, k, at, low, high in windows:
        y = turn(q_ref[group, k, low:high], work[at : at + WIN, cols])
        work[at + low : at + high, cols] = y


def tile_order(own):
    tiles = (own + 1) // 2
    return [0, tiles - 2] + list(range(1, tiles - 2)) + [tiles - 1]


def back_kernel(
    own, rows_axis, cols_axis, refl_ref, x_ref, out_ref,
    q_ref, work, raw, edge, beside, slab, ex, relayed, late,
    near_send, near_recv, line_send, line_recv, pair_send, pair_recv, halo_send, halo_recv, own_sem, x_sem,
):
    row, me = lax.axis_index("row"), lax.axis_index("col")
    chips = cols_axis // 2
    chip, core = me // 2, me % 2
    up, down = (row + rows_axis - 1) % rows_axis, (row + 1) % rows_axis
    other = chip * 2 + 1 - core
    rows, columns = x_ref.shape
    stored = raw.shape[1]
    order = tile_order(own)
    share_group = cols_axis // GROUPS
    group_of = me // share_group
    two = 2 * share_group
    has_up, has_down = row > 0, row < rows_axis - 1
    mesh_ids = pl.DeviceIdType.MESH
    no = jnp.logical_not
    detour = rows_axis == 4
    across = (row + 2) % rows_axis

    def remote(source, target, send, recv, device):
        return pltpu.make_async_remote_copy(
            src_ref=source, dst_ref=target, send_sem=send, recv_sem=recv,
            device_id=device, device_id_type=mesh_ids,
        )

    local = pltpu.make_async_copy(refl_ref, raw, own_sem)
    local.start()
    fill = pltpu.make_async_copy(x_ref, work.at[pl.ds(HALO, rows)], x_sem)
    fill.start()
    first, third = group_of == 0, group_of == 2
    barrier = pltpu.get_barrier_semaphore()
    partners = [(row, mixed(chip, i, chips) * 2 + core) for i in range(1, chips)]
    partners += [(row, other), (up, me), (down, me)]
    if detour:
        partners.append((across, me))

    def greet(partner):
        pl.semaphore_signal(barrier, inc=1, device_id=partner, device_id_type=mesh_ids)

    for partner in partners:
        greet(partner)
    pl.when(first)(lambda: greet((up, (me + two) % cols_axis)))
    pl.when(third)(lambda: greet((down, (me + cols_axis - two) % cols_axis)))

    @pl.when(no(has_up))
    def _():
        work[0:HALO] = jnp.zeros((HALO, columns), jnp.float32)
        ex[0] = jnp.zeros((BAND, columns), jnp.float32)

    @pl.when(no(has_down))
    def _():
        work[HALO + rows :] = jnp.zeros((HALO, columns), jnp.float32)
        ex[1] = jnp.zeros((BAND, columns), jnp.float32)

    gets_near = jnp.where(third, has_down, has_up)

    @pl.when(no(gets_near))
    def _():
        beside[...] = jnp.zeros(beside.shape, jnp.float32)

    local.wait()
    edge[:, :BAND] = raw[:, stored - BAND :]
    edge[:, BAND:] = jnp.zeros((raw.shape[0], BAND), jnp.float32)
    for at, tile in enumerate(order[:-1]):
        slab[me, :, at * WIN : (at + 1) * WIN] = raw[:, tile * WIN : (tile + 1) * WIN]
    pl.semaphore_wait(barrier, len(partners) + jnp.where(first | third, 1, 0))

    last = (len(order) - 1) * WIN
    spans = (pl.ds(0, 2 * WIN), pl.ds(last, WIN), pl.ds(2 * WIN, last - 2 * WIN))
    tail = remote(edge, beside, near_send.at[0], near_recv.at[0], (down, me))
    head = remote(slab.at[me, :, pl.ds(0, WIN)], beside, near_send.at[1], near_recv.at[0], (up, (me + two) % cols_axis))
    sends_tail = has_down & no(third)
    sends_head = has_up & first
    pl.when(sends_tail)(tail.start)
    pl.when(sends_head)(head.start)
    pending = []

    def share_pair(kind):
        part = slab.at[me, :, spans[kind]]
        pair = remote(part, part, pair_send.at[kind, chip], pair_recv.at[kind, chip], (row, other))
        pair.start()
        pending.append(pair)

    def share_line(kind, reach):
        part = slab.at[me, :, spans[kind]]
        for i in reach:
            there = mixed(chip, i, chips)
            line = remote(part, part, line_send.at[kind, there], line_recv.at[kind, chip], (row, there * 2 + core))
            line.start()
            pending.append(line)

    chip_group = share_group // 2
    mine = chip // chip_group
    all_chips = range(1, chips)

    def exchange(at, down_from, up_from, top, bottom, held):
        half = columns // 2
        left, right = pl.ds(0, half), pl.ds(half, half)
        send, recv = halo_send.at[at], halo_recv.at[at]

        def flow(index, source, target, cols, device):
            return remote(source.at[:, cols], target.at[:, cols], send.at[index], recv.at[index], device)

        above = [flow(0, down_from, top, left, (down, me)), flow(1, down_from, top, right, (down, me))]
        below = [flow(2, up_from, bottom, left, (up, me)), flow(3, up_from, bottom, right, (up, me))]
        starts = []
        relays = []
        if detour:
            starts.append((row == 1, remote(down_from.at[:, right], held, send.at[1], recv.at[4], (across, me))))
            starts.append((row == 2, remote(up_from.at[:, right], held, send.at[3], recv.at[4], (across, me))))
            relays.append((row == 3, remote(held, top.at[:, right], send.at[4], recv.at[1], (up, me))))
            relays.append((row == 0, remote(held, bottom.at[:, right], send.at[4], recv.at[3], (down, me))))
        starts.append((has_down & (row != 1) if detour else has_down, above[1]))
        starts.append((has_up & (row != 2) if detour else has_up, below[1]))
        parts = [[(has_down, above[0]), (has_up, below[0])], starts]

        def start(half):
            for here, copy in parts[half]:
                pl.when(here)(copy.start)

        def relay():
            for here, copy in relays:
                arrival = remote(held, held, send.at[4], recv.at[4], (across, me))

                @pl.when(here)
                def _():
                    arrival.wait_recv()
                    copy.start()

        def wait_recv(half):
            pl.when(has_up)(above[half].wait_recv)
            pl.when(has_down)(below[half].wait_recv)

        def wait_send():
            for here, copy in parts[0] + parts[1] + relays:
                pl.when(here)(copy.wait_send)

        return start, relay, wait_recv, wait_send

    early = exchange(
        0, x_ref.at[pl.ds(rows - HALO, HALO)], x_ref.at[pl.ds(0, HALO)],
        work.at[pl.ds(0, HALO)], work.at[pl.ds(HALO + rows, HALO)], relayed,
    )
    final = exchange(
        1, work.at[pl.ds(HALO + rows - BAND, BAND)], work.at[pl.ds(HALO, BAND)], ex.at[0], ex.at[1], late,
    )

    def forward(kind, reach):
        for i in reach:
            there = mixed(chip, i, chips)
            slot = slab.at[there * 2 + core, :, spans[kind]]
            copy = remote(slot, slot, pair_send.at[kind, there], pair_recv.at[kind, there], (row, other))
            remote(slot, slot, own_sem, line_recv.at[kind, there], (row, other)).wait_recv()
            copy.start()
            pending.append(copy)

    def landed(kind, reach):
        for i in reach:
            there = mixed(chip, i, chips)
            slot = slab.at[there * 2 + 1 - core, :, spans[kind]]
            remote(slot, slot, own_sem, pair_recv.at[kind, there], (row, other)).wait_recv()

    def taken(group, at):
        part = slab[pl.ds(group * share_group, share_group), :, pl.ds(at, WIN)]
        return part.reshape(BAND, WIN)

    def build(pairs):
        picks = []
        for sides in pairs:
            parts = [taken(group, order.index(tile) * WIN) for group, tile in sides]
            slots = [(group, 2 * tile + half) for half, (group, tile) in enumerate(sides)]
            picks.append((parts, slots))
        build_windows(own, rows_axis, picks, q_ref)

    tiles = len(order)
    others = [mixed(mine, i, GROUPS) for i in range(1, GROUPS)]
    inside, beyond = range(1, chip_group), range(chip_group, 2 * chip_group)
    near_by, far_off = range(1, 2 * chip_group), range(2 * chip_group, chips)
    share_pair(0)
    share_pair(2)
    share_line(0, near_by)
    share_line(2, near_by)
    share_line(0, far_off)
    early[0](1)
    early[0](0)
    for kind in (0, 2):
        forward(kind, inside)
    for kind in (0, 2):
        landed(kind, range(chip_group))
    build([((mine, tile),) * 2 for tile in range(tiles - 1)])
    pl.when(gets_near)(tail.wait_recv)
    slab[me, :, last:] = jnp.where(
        lax.broadcasted_iota(jnp.int32, edge.shape, 1) < BAND, edge[...], pltpu.roll(beside[...], BAND, 1)
    )
    share_pair(1)
    share_line(1, all_chips)
    early[1]()
    share_line(2, far_off)
    for kind in (0, 2):
        forward(kind, beyond)
    for kind in (0, 2):
        landed(kind, beyond)
    build([((others[0], tile),) * 2 for tile in range(tiles - 1)])
    forward(0, far_off)
    forward(1, all_chips)
    landed(0, far_off)
    landed(1, range(chips))
    ends = [(group, tile) for tile in (0, tiles - 2) for group in others[1:]]
    ends += [(group, tiles - 1) for group in [mine] + others]
    build([(pair, pair) for pair in ends])

    def window(group, k):
        return group, k, HALO + BAND * (group % 2) + WIN * k, 0, WIN

    edges = [
        (0, own, 0, BAND, WIN),
        window(0, 0),
        window(0, 1),
        window(0, own - 2),
        window(0, own - 1),
        (2, own, HALO + rows, 0, BAND),
        (1, own, HALO - BAND, BAND, WIN),
        window(1, 0),
        window(1, own - 2),
        (1, own - 1, HALO + rows - BAND, 0, BAND),
        window(2, 0),
        window(2, own - 1),
    ]
    inner = [window(0, k) for k in range(2, own - 2)]
    inner += [window(1, k) for k in range(1, own - 2)]
    inner += [window(2, k) for k in range(1, own - 1)]

    fill.wait()
    forward(2, far_off)
    halves = [pl.ds(half * (columns // 2), columns // 2) for half in range(2)]
    for half in (1, 0):
        early[2](half)
        apply_windows(edges, q_ref, work, halves[half])
        final[0](half)
    landed(2, far_off)
    build([((group, tile),) * 2 for tile in range(1, tiles - 2) for group in others[1:]])
    final[1]()
    for half in halves:
        apply_windows(inner, q_ref, work, half)

    def finish(cols):
        for k in range(own - 1):
            at = BAND + WIN * k
            out_ref[at : at + WIN, cols] = turn(q_ref[3, k], work[HALO + at : HALO + at + WIN, cols])

    for half in halves:
        finish(half)

    def straddle(cols):
        x = jnp.concatenate([ex[0, :, cols], work[HALO : HALO + BAND, cols]], 0)
        out_ref[:BAND, cols] = turn(q_ref[3, own, BAND:], x)
        x = jnp.concatenate([work[HALO + rows - BAND : HALO + rows, cols], ex[1, :, cols]], 0)
        out_ref[rows - BAND :, cols] = turn(q_ref[3, own - 1, :BAND], x)

    for half in (0, 1):
        final[2](half)
        straddle(halves[half])
    pl.when(sends_tail)(tail.wait_send)
    pl.when(sends_head)(head.wait_send)
    early[3]()
    final[3]()
    for copy in pending:
        copy.wait_send()


def shards(vectors, reflectors):
    rows, columns = vectors.shape
    own = rows // WIN
    rows_axis, cols_axis = lax.axis_size("row"), lax.axis_size("col")
    slots, stored = reflectors.shape
    chips = cols_axis // 2
    dma = pltpu.SemaphoreType.DMA
    return pl.pallas_call(
        functools.partial(back_kernel, own, rows_axis, cols_axis),
        in_specs=[pl.BlockSpec(memory_space=pltpu.HBM)] * 2,
        out_specs=pl.BlockSpec(memory_space=pltpu.VMEM),
        out_shape=jax.ShapeDtypeStruct(vectors.shape, vectors.dtype),
        scratch_shapes=[
            pltpu.VMEM((GROUPS, own + 1, WIN, 2 * WIN), jnp.bfloat16),
            pltpu.VMEM((rows + 2 * HALO, columns), jnp.float32),
            pltpu.VMEM((slots, stored), jnp.float32),
            pltpu.VMEM((slots, WIN), jnp.float32),
            pltpu.VMEM((slots, WIN), jnp.float32),
            pltpu.VMEM((cols_axis, slots, stored + BAND), jnp.float32),
            pltpu.VMEM((2, BAND, columns), jnp.float32),
            pltpu.VMEM((HALO, columns // 2), jnp.float32),
            pltpu.VMEM((BAND, columns // 2), jnp.float32),
            dma((2,)),
            dma((1,)),
            dma((3, chips)),
            dma((3, chips)),
            dma((3, chips)),
            dma((3, chips)),
            dma((2, 5)),
            dma((2, 5)),
            dma,
            dma,
        ],
        compiler_params=pltpu.CompilerParams(collective_id=0, has_side_effects=True, vmem_limit_bytes=50 * 2**20),
        name="back",
    )(reflectors, vectors)


def solution(mesh):
    placed = (P("row", "col"), P("col", "row"))
    return jax.shard_map(
        shards, mesh=mesh, in_specs=placed, out_specs=P("row", "col"), check_vma=False
    )
```

```python
import functools

import jax
import jax.numpy as jnp
from jax import lax
from jax.experimental import pallas as pl
from jax.experimental.pallas import tpu as pltpu
from jax.sharding import PartitionSpec as P

BAND = 64
GROUPS = 4
WIN = 2 * BAND
HALO = 2 * BAND


def split(x):
    high = x.astype(jnp.bfloat16)
    low = (x - high.astype(jnp.float32)).astype(jnp.bfloat16)
    return high, low


def dot(a, b, dims=(1, 0)):
    return lax.dot_general(
        a, b, (((dims[0],), (dims[1],)), ((), ())), preferred_element_type=jnp.float32
    )


def product(a, b):
    ah, al = split(a)
    bh, bl = split(b)
    return dot(jnp.concatenate([ah, al, ah], 1), jnp.concatenate([bh, bh, bl], 0))


def keep(q, q_ref, group, k):
    high, low = split(q)
    q_ref[group, k, :, :WIN] = high
    q_ref[group, k, :, WIN:] = low


def build_windows(own, rows_axis, picks, q_ref):
    grid_row = lax.axis_index("row")
    size = WIN
    row = lax.broadcasted_iota(jnp.int32, (size, size), 0)
    lane = lax.broadcasted_iota(jnp.int32, (size, size), 1)
    eye = row == lane
    identity = eye.astype(jnp.float32)
    upper = (row // BAND == lane // BAND) & (row < lane)
    inside = (row // BAND) == (lane // BAND)
    lead = inside & (lane % BAND == 0)

    skews, nils, invs, scaled = [], [], [], []
    for (left, right), _ in picks:
        both = jnp.concatenate([left, right], 0)
        both = jnp.where(lead, 1.0, jnp.where(inside, both, 0.0))
        skews.append(pltpu.roll(both, 0, 1, stride=1, stride_axis=0))
    for skew in skews:
        high, low = split(skew)
        gram = dot(
            jnp.concatenate([high, low, high], 1), jnp.concatenate([high, high, low], 1), (1, 1)
        )
        diag = 0.5 * jnp.sum(jnp.where(eye, gram, 0.0), axis=1, keepdims=True)
        scale = 1.0 / diag
        nils.append(jnp.where(upper, gram * scale, 0.0))
        scaled.append(skew * scale)
    block = BAND // 4
    near = row // block == lane // block
    powers = [jnp.where(near, n, 0.0) for n in nils]
    invs = [identity - p for p in powers]
    powers = [product(p, p) for p in powers]
    for level in range(2):
        stacked = [product(jnp.concatenate([i, p], 0), p) for i, p in zip(invs, powers)]
        invs = [i + s[:size] for i, s in zip(invs, stacked)]
        powers = [s[size:] for s in stacked]
    invs = [i + product(i, p) for i, p in zip(invs, powers)]
    for _ in range(2):
        wide = row // (2 * block) == lane // (2 * block)
        far = wide & (row // block != lane // block)
        cross = [product(jnp.where(far, n, 0.0), i) for n, i in zip(nils, invs)]
        invs = [i - product(i, c) for i, c in zip(invs, cross)]
        block *= 2
    solved = [product(i, s) for i, s in zip(invs, scaled)]
    for (_, slots), skew, wing in zip(picks, skews, solved):
        sh, sl = split(skew)
        th, tl = split(wing)
        for half, (group, k) in enumerate(slots):
            own_rows = slice(half * BAND, (half + 1) * BAND)
            left = jnp.concatenate([sh[own_rows], sl[own_rows], sh[own_rows]], 0)
            right = jnp.concatenate([th[own_rows], th[own_rows], tl[own_rows]], 0)
            change = dot(left, right, (0, 0))
            outer = jnp.where(group == 2, grid_row < rows_axis - 1, grid_row > 0)
            inner = grid_row * own + k < own * rows_axis - group % 2
            q = identity - jnp.where(jnp.where(k == own, outer, inner), change, 0.0)
            keep(q, q_ref, group, k)


def mixed(a, b, count):
    total, bit = 0, 1
    while bit < count:
        total = total + ((a // bit + b // bit) % 2) * bit
        bit *= 2
    return total


def turn(q, x):
    xh, xl = split(x)
    return dot(q, jnp.concatenate([xh, xh], 0)) + dot(q[:, :WIN], xl)


def apply_windows(windows, q_ref, work, cols):
    for group, k, at, low, high in windows:
        y = turn(q_ref[group, k, low:high], work[at : at + WIN, cols])
        work[at + low : at + high, cols] = y


def tile_order(own):
    tiles = (own + 1) // 2
    return [0, tiles - 2] + list(range(1, tiles - 2)) + [tiles - 1]


def back_kernel(
    own, rows_axis, cols_axis, refl_ref, x_ref, out_ref,
    q_ref, work, raw, edge, beside, slab, ex, relayed, late,
    near_send, near_recv, line_send, line_recv, pair_send, pair_recv, halo_send, halo_recv, own_sem, x_sem,
):
    row, me = lax.axis_index("row"), lax.axis_index("col")
    chips = cols_axis // 2
    chip, core = me // 2, me % 2
    up, down = (row + rows_axis - 1) % rows_axis, (row + 1) % rows_axis
    other = chip * 2 + 1 - core
    rows, columns = x_ref.shape
    stored = raw.shape[1]
    order = tile_order(own)
    share_group = cols_axis // GROUPS
    group_of = me // share_group
    two = 2 * share_group
    has_up, has_down = row > 0, row < rows_axis - 1
    mesh_ids = pl.DeviceIdType.MESH
    no = jnp.logical_not
    detour = rows_axis == 4
    across = (row + 2) % rows_axis

    def remote(source, target, send, recv, device):
        return pltpu.make_async_remote_copy(
            src_ref=source, dst_ref=target, send_sem=send, recv_sem=recv,
            device_id=device, device_id_type=mesh_ids,
        )

    local = pltpu.make_async_copy(refl_ref, raw, own_sem)
    local.start()
    fill = pltpu.make_async_copy(x_ref, work.at[pl.ds(HALO, rows)], x_sem)
    fill.start()
    first, third = group_of == 0, group_of == 2
    barrier = pltpu.get_barrier_semaphore()
    partners = [(row, mixed(chip, i, chips) * 2 + core) for i in range(1, chips)]
    partners += [(row, other), (up, me), (down, me)]
    if detour:
        partners.append((across, me))

    def greet(partner):
        pl.semaphore_signal(barrier, inc=1, device_id=partner, device_id_type=mesh_ids)

    for partner in partners:
        greet(partner)
    pl.when(first)(lambda: greet((up, (me + two) % cols_axis)))
    pl.when(third)(lambda: greet((down, (me + cols_axis - two) % cols_axis)))

    @pl.when(no(has_up))
    def _():
        work[0:HALO] = jnp.zeros((HALO, columns), jnp.float32)
        ex[0] = jnp.zeros((BAND, columns), jnp.float32)

    @pl.when(no(has_down))
    def _():
        work[HALO + rows :] = jnp.zeros((HALO, columns), jnp.float32)
        ex[1] = jnp.zeros((BAND, columns), jnp.float32)

    gets_near = jnp.where(third, has_down, has_up)

    @pl.when(no(gets_near))
    def _():
        beside[...] = jnp.zeros(beside.shape, jnp.float32)

    local.wait()
    edge[:, :BAND] = raw[:, stored - BAND :]
    edge[:, BAND:] = jnp.zeros((raw.shape[0], BAND), jnp.float32)
    for at, tile in enumerate(order[:-1]):
        slab[me, :, at * WIN : (at + 1) * WIN] = raw[:, tile * WIN : (tile + 1) * WIN]
    pl.semaphore_wait(barrier, len(partners) + jnp.where(first | third, 1, 0))

    last = (len(order) - 1) * WIN
    spans = (pl.ds(0, 2 * WIN), pl.ds(last, WIN), pl.ds(2 * WIN, last - 2 * WIN))
    tail = remote(edge, beside, near_send.at[0], near_recv.at[0], (down, me))
    head = remote(slab.at[me, :, pl.ds(0, WIN)], beside, near_send.at[1], near_recv.at[0], (up, (me + two) % cols_axis))
    sends_tail = has_down & no(third)
    sends_head = has_up & first
    pl.when(sends_tail)(tail.start)
    pl.when(sends_head)(head.start)
    pending = []

    def share_pair(kind):
        part = slab.at[me, :, spans[kind]]
        pair = remote(part, part, pair_send.at[kind, chip], pair_recv.at[kind, chip], (row, other))
        pair.start()
        pending.append(pair)

    def share_line(kind, reach):
        part = slab.at[me, :, spans[kind]]
        for i in reach:
            there = mixed(chip, i, chips)
            line = remote(part, part, line_send.at[kind, there], line_recv.at[kind, chip], (row, there * 2 + core))
            line.start()
            pending.append(line)

    chip_group = share_group // 2
    mine = chip // chip_group
    all_chips = range(1, chips)

    def exchange(at, down_from, up_from, top, bottom, held):
        half = columns // 2
        left, right = pl.ds(0, half), pl.ds(half, half)
        send, recv = halo_send.at[at], halo_recv.at[at]

        def flow(index, source, target, cols, device):
            return remote(source.at[:, cols], target.at[:, cols], send.at[index], recv.at[index], device)

        above = [flow(0, down_from, top, left, (down, me)), flow(1, down_from, top, right, (down, me))]
        below = [flow(2, up_from, bottom, left, (up, me)), flow(3, up_from, bottom, right, (up, me))]
        starts = []
        relays = []
        if detour:
            starts.append((row == 1, remote(down_from.at[:, right], held, send.at[1], recv.at[4], (across, me))))
            starts.append((row == 2, remote(up_from.at[:, right], held, send.at[3], recv.at[4], (across, me))))
            relays.append((row == 3, remote(held, top.at[:, right], send.at[4], recv.at[1], (up, me))))
            relays.append((row == 0, remote(held, bottom.at[:, right], send.at[4], recv.at[3], (down, me))))
        starts.append((has_down & (row != 1) if detour else has_down, above[1]))
        starts.append((has_up & (row != 2) if detour else has_up, below[1]))
        parts = [[(has_down, above[0]), (has_up, below[0])], starts]

        def start(half):
            for here, copy in parts[half]:
                pl.when(here)(copy.start)

        def relay():
            for here, copy in relays:
                arrival = remote(held, held, send.at[4], recv.at[4], (across, me))

                @pl.when(here)
                def _():
                    arrival.wait_recv()
                    copy.start()

        def wait_recv(half):
            pl.when(has_up)(above[half].wait_recv)
            pl.when(has_down)(below[half].wait_recv)

        def wait_send():
            for here, copy in parts[0] + parts[1] + relays:
                pl.when(here)(copy.wait_send)

        return start, relay, wait_recv, wait_send

    early = exchange(
        0, x_ref.at[pl.ds(rows - HALO, HALO)], x_ref.at[pl.ds(0, HALO)],
        work.at[pl.ds(0, HALO)], work.at[pl.ds(HALO + rows, HALO)], relayed,
    )
    final = exchange(
        1, work.at[pl.ds(HALO + rows - BAND, BAND)], work.at[pl.ds(HALO, BAND)], ex.at[0], ex.at[1], late,
    )

    def forward(kind, reach):
        for i in reach:
            there = mixed(chip, i, chips)
            slot = slab.at[there * 2 + core, :, spans[kind]]
            copy = remote(slot, slot, pair_send.at[kind, there], pair_recv.at[kind, there], (row, other))
            remote(slot, slot, own_sem, line_recv.at[kind, there], (row, other)).wait_recv()
            copy.start()
            pending.append(copy)

    def landed(kind, reach):
        for i in reach:
            there = mixed(chip, i, chips)
            slot = slab.at[there * 2 + 1 - core, :, spans[kind]]
            remote(slot, slot, own_sem, pair_recv.at[kind, there], (row, other)).wait_recv()

    def taken(group, at):
        part = slab[pl.ds(group * share_group, share_group), :, pl.ds(at, WIN)]
        return part.reshape(BAND, WIN)

    def build(pairs):
        picks = []
        for sides in pairs:
            parts = [taken(group, order.index(tile) * WIN) for group, tile in sides]
            slots = [(group, 2 * tile + half) for half, (group, tile) in enumerate(sides)]
            picks.append((parts, slots))
        build_windows(own, rows_axis, picks, q_ref)

    tiles = len(order)
    others = [mixed(mine, i, GROUPS) for i in range(1, GROUPS)]
    inside, beyond = range(1, chip_group), range(chip_group, 2 * chip_group)
    near_by, far_off = range(1, 2 * chip_group), range(2 * chip_group, chips)
    share_pair(0)
    share_pair(2)
    share_line(0, near_by)
    share_line(2, near_by)
    share_line(0, far_off)
    early[0](1)
    early[0](0)
    for kind in (0, 2):
        forward(kind, inside)
    for kind in (0, 2):
        landed(kind, range(chip_group))
    build([((mine, tile),) * 2 for tile in range(tiles - 1)])
    pl.when(gets_near)(tail.wait_recv)
    slab[me, :, last:] = jnp.where(
        lax.broadcasted_iota(jnp.int32, edge.shape, 1) < BAND, edge[...], pltpu.roll(beside[...], BAND, 1)
    )
    share_pair(1)
    share_line(1, all_chips)
    early[1]()
    for kind in (0, 2):
        forward(kind, beyond)
    for kind in (0, 2):
        landed(kind, beyond)
    build([((others[0], tile),) * 2 for tile in range(tiles - 1)])
    share_line(2, far_off)
    forward(0, far_off)
    forward(1, all_chips)
    landed(0, far_off)
    landed(1, range(chips))
    ends = [(group, tile) for tile in (0, tiles - 2) for group in others[1:]]
    ends += [(group, tiles - 1) for group in range(GROUPS - 1)]
    build([(pair, pair) for pair in ends])

    def window(group, k):
        return group, k, HALO + BAND * (group % 2) + WIN * k, 0, WIN

    edges = [
        (0, own, 0, BAND, WIN),
        window(0, 0),
        window(0, 1),
        window(0, own - 2),
        window(0, own - 1),
        (2, own, HALO + rows, 0, BAND),
        (1, own, HALO - BAND, BAND, WIN),
        window(1, 0),
        window(1, own - 2),
        (1, own - 1, HALO + rows - BAND, 0, BAND),
        window(2, 0),
        window(2, own - 1),
    ]
    inner = [window(0, k) for k in range(2, own - 2)]
    inner += [window(1, k) for k in range(1, own - 2)]
    inner += [window(2, k) for k in range(1, own - 1)]

    fill.wait()
    forward(2, far_off)
    halves = [pl.ds(half * (columns // 2), columns // 2) for half in range(2)]
    for half in (1, 0):
        early[2](half)
        apply_windows(edges, q_ref, work, halves[half])
        final[0](half)
    landed(2, far_off)
    under = [(group, tile) for tile in range(1, tiles - 2) for group in others[1:]]
    build([(pair, pair) for pair in under + [(GROUPS - 1, tiles - 1)]])
    final[1]()
    for half in halves:
        apply_windows(inner, q_ref, work, half)

    def finish(cols):
        for k in range(own - 1):
            at = BAND + WIN * k
            out_ref[at : at + WIN, cols] = turn(q_ref[3, k], work[HALO + at : HALO + at + WIN, cols])

    for half in halves:
        finish(half)

    def straddle(cols):
        x = jnp.concatenate([ex[0, :, cols], work[HALO : HALO + BAND, cols]], 0)
        out_ref[:BAND, cols] = turn(q_ref[3, own, BAND:], x)
        x = jnp.concatenate([work[HALO + rows - BAND : HALO + rows, cols], ex[1, :, cols]], 0)
        out_ref[rows - BAND :, cols] = turn(q_ref[3, own - 1, :BAND], x)

    for half in (0, 1):
        final[2](half)
        straddle(halves[half])
    pl.when(sends_tail)(tail.wait_send)
    pl.when(sends_head)(head.wait_send)
    early[3]()
    final[3]()
    for copy in pending:
        copy.wait_send()


def shards(vectors, reflectors):
    rows, columns = vectors.shape
    own = rows // WIN
    rows_axis, cols_axis = lax.axis_size("row"), lax.axis_size("col")
    slots, stored = reflectors.shape
    chips = cols_axis // 2
    dma = pltpu.SemaphoreType.DMA
    return pl.pallas_call(
        functools.partial(back_kernel, own, rows_axis, cols_axis),
        in_specs=[pl.BlockSpec(memory_space=pltpu.HBM)] * 2,
        out_specs=pl.BlockSpec(memory_space=pltpu.VMEM),
        out_shape=jax.ShapeDtypeStruct(vectors.shape, vectors.dtype),
        scratch_shapes=[
            pltpu.VMEM((GROUPS, own + 1, WIN, 2 * WIN), jnp.bfloat16),
            pltpu.VMEM((rows + 2 * HALO, columns), jnp.float32),
            pltpu.VMEM((slots, stored), jnp.float32),
            pltpu.VMEM((slots, WIN), jnp.float32),
            pltpu.VMEM((slots, WIN), jnp.float32),
            pltpu.VMEM((cols_axis, slots, stored + BAND), jnp.float32),
            pltpu.VMEM((2, BAND, columns), jnp.float32),
            pltpu.VMEM((HALO, columns // 2), jnp.float32),
            pltpu.VMEM((BAND, columns // 2), jnp.float32),
            dma((2,)),
            dma((1,)),
            dma((3, chips)),
            dma((3, chips)),
            dma((3, chips)),
            dma((3, chips)),
            dma((2, 5)),
            dma((2, 5)),
            dma,
            dma,
        ],
        compiler_params=pltpu.CompilerParams(collective_id=0, has_side_effects=True, vmem_limit_bytes=50 * 2**20),
        name="back",
    )(reflectors, vectors)


def solution(mesh):
    placed = (P("row", "col"), P("col", "row"))
    return jax.shard_map(
        shards, mesh=mesh, in_specs=placed, out_specs=P("row", "col"), check_vma=False
    )
```

```python
import functools

import jax
import jax.numpy as jnp
from jax import lax
from jax.experimental import pallas as pl
from jax.experimental.pallas import tpu as pltpu
from jax.sharding import PartitionSpec as P

BAND = 64
GROUPS = 4
WIN = 2 * BAND
HALO = 2 * BAND


def split(x):
    high = x.astype(jnp.bfloat16)
    low = (x - high.astype(jnp.float32)).astype(jnp.bfloat16)
    return high, low


def dot(a, b, dims=(1, 0)):
    return lax.dot_general(
        a, b, (((dims[0],), (dims[1],)), ((), ())), preferred_element_type=jnp.float32
    )


def product(a, b):
    ah, al = split(a)
    bh, bl = split(b)
    return dot(jnp.concatenate([ah, al, ah], 1), jnp.concatenate([bh, bh, bl], 0))


def keep(q, q_ref, group, k):
    high, low = split(q)
    q_ref[group, k, :, :WIN] = high
    q_ref[group, k, :, WIN:] = low


def build_windows(own, rows_axis, picks, q_ref):
    grid_row = lax.axis_index("row")
    size = WIN
    row = lax.broadcasted_iota(jnp.int32, (size, size), 0)
    lane = lax.broadcasted_iota(jnp.int32, (size, size), 1)
    eye = row == lane
    identity = eye.astype(jnp.float32)
    upper = (row // BAND == lane // BAND) & (row < lane)
    inside = (row // BAND) == (lane // BAND)
    lead = inside & (lane % BAND == 0)

    skews, nils, invs, scaled = [], [], [], []
    for (left, right), _ in picks:
        both = jnp.concatenate([left, right], 0)
        both = jnp.where(lead, 1.0, jnp.where(inside, both, 0.0))
        skews.append(pltpu.roll(both, 0, 1, stride=1, stride_axis=0))
    for skew in skews:
        high, low = split(skew)
        gram = dot(
            jnp.concatenate([high, low, high], 1), jnp.concatenate([high, high, low], 1), (1, 1)
        )
        diag = 0.5 * jnp.sum(jnp.where(eye, gram, 0.0), axis=1, keepdims=True)
        scale = 1.0 / diag
        nils.append(jnp.where(upper, gram * scale, 0.0))
        scaled.append(skew * scale)
    block = BAND // 4
    near = row // block == lane // block
    powers = [jnp.where(near, n, 0.0) for n in nils]
    invs = [identity - p for p in powers]
    powers = [product(p, p) for p in powers]
    for level in range(2):
        stacked = [product(jnp.concatenate([i, p], 0), p) for i, p in zip(invs, powers)]
        invs = [i + s[:size] for i, s in zip(invs, stacked)]
        powers = [s[size:] for s in stacked]
    invs = [i + product(i, p) for i, p in zip(invs, powers)]
    for _ in range(2):
        wide = row // (2 * block) == lane // (2 * block)
        far = wide & (row // block != lane // block)
        cross = [product(jnp.where(far, n, 0.0), i) for n, i in zip(nils, invs)]
        invs = [i - product(i, c) for i, c in zip(invs, cross)]
        block *= 2
    solved = [product(i, s) for i, s in zip(invs, scaled)]
    for (_, slots), skew, wing in zip(picks, skews, solved):
        sh, sl = split(skew)
        th, tl = split(wing)
        for half, (group, k) in enumerate(slots):
            own_rows = slice(half * BAND, (half + 1) * BAND)
            left = jnp.concatenate([sh[own_rows], sl[own_rows], sh[own_rows]], 0)
            right = jnp.concatenate([th[own_rows], th[own_rows], tl[own_rows]], 0)
            change = dot(left, right, (0, 0))
            outer = jnp.where(group == 2, grid_row < rows_axis - 1, grid_row > 0)
            inner = grid_row * own + k < own * rows_axis - group % 2
            q = identity - jnp.where(jnp.where(k == own, outer, inner), change, 0.0)
            keep(q, q_ref, group, k)


def mixed(a, b, count):
    total, bit = 0, 1
    while bit < count:
        total = total + ((a // bit + b // bit) % 2) * bit
        bit *= 2
    return total


def turn(q, x):
    xh, xl = split(x)
    return dot(q, jnp.concatenate([xh, xh], 0)) + dot(q[:, :WIN], xl)


def apply_windows(windows, q_ref, work, cols):
    for group, k, at, low, high in windows:
        y = turn(q_ref[group, k, low:high], work[at : at + WIN, cols])
        work[at + low : at + high, cols] = y


def tile_order(own):
    tiles = (own + 1) // 2
    return [0, tiles - 2] + list(range(1, tiles - 2)) + [tiles - 1]


def back_kernel(
    own, rows_axis, cols_axis, refl_ref, x_ref, out_ref,
    q_ref, work, raw, edge, beside, slab, ex, relayed, late,
    near_send, near_recv, line_send, line_recv, pair_send, pair_recv, halo_send, halo_recv, own_sem, x_sem,
):
    row, me = lax.axis_index("row"), lax.axis_index("col")
    chips = cols_axis // 2
    chip, core = me // 2, me % 2
    up, down = (row + rows_axis - 1) % rows_axis, (row + 1) % rows_axis
    other = chip * 2 + 1 - core
    rows, columns = x_ref.shape
    stored = raw.shape[1]
    order = tile_order(own)
    share_group = cols_axis // GROUPS
    group_of = me // share_group
    two = 2 * share_group
    has_up, has_down = row > 0, row < rows_axis - 1
    mesh_ids = pl.DeviceIdType.MESH
    no = jnp.logical_not
    detour = rows_axis == 4
    across = (row + 2) % rows_axis

    def remote(source, target, send, recv, device):
        return pltpu.make_async_remote_copy(
            src_ref=source, dst_ref=target, send_sem=send, recv_sem=recv,
            device_id=device, device_id_type=mesh_ids,
        )

    local = pltpu.make_async_copy(refl_ref, raw, own_sem)
    local.start()
    fill = pltpu.make_async_copy(x_ref, work.at[pl.ds(HALO, rows)], x_sem)
    fill.start()
    first, third = group_of == 0, group_of == 2
    barrier = pltpu.get_barrier_semaphore()
    partners = [(row, mixed(chip, i, chips) * 2 + core) for i in range(1, chips)]
    partners += [(row, other), (up, me), (down, me)]
    if detour:
        partners.append((across, me))

    def greet(partner):
        pl.semaphore_signal(barrier, inc=1, device_id=partner, device_id_type=mesh_ids)

    for partner in partners:
        greet(partner)
    pl.when(first)(lambda: greet((up, (me + two) % cols_axis)))
    pl.when(third)(lambda: greet((down, (me + cols_axis - two) % cols_axis)))

    @pl.when(no(has_up))
    def _():
        work[0:HALO] = jnp.zeros((HALO, columns), jnp.float32)
        ex[0] = jnp.zeros((BAND, columns), jnp.float32)

    @pl.when(no(has_down))
    def _():
        work[HALO + rows :] = jnp.zeros((HALO, columns), jnp.float32)
        ex[1] = jnp.zeros((BAND, columns), jnp.float32)

    gets_near = jnp.where(third, has_down, has_up)

    @pl.when(no(gets_near))
    def _():
        beside[...] = jnp.zeros(beside.shape, jnp.float32)

    local.wait()
    edge[:, :BAND] = raw[:, stored - BAND :]
    edge[:, BAND:] = jnp.zeros((raw.shape[0], BAND), jnp.float32)
    for at, tile in enumerate(order[:-1]):
        slab[me, :, at * WIN : (at + 1) * WIN] = raw[:, tile * WIN : (tile + 1) * WIN]
    pl.semaphore_wait(barrier, len(partners) + jnp.where(first | third, 1, 0))

    last = (len(order) - 1) * WIN
    spans = (pl.ds(0, 2 * WIN), pl.ds(last, WIN), pl.ds(2 * WIN, last - 2 * WIN))
    tail = remote(edge, beside, near_send.at[0], near_recv.at[0], (down, me))
    head = remote(slab.at[me, :, pl.ds(0, WIN)], beside, near_send.at[1], near_recv.at[0], (up, (me + two) % cols_axis))
    sends_tail = has_down & no(third)
    sends_head = has_up & first
    pl.when(sends_tail)(tail.start)
    pl.when(sends_head)(head.start)
    pending = []

    def share_pair(kind):
        part = slab.at[me, :, spans[kind]]
        pair = remote(part, part, pair_send.at[kind, chip], pair_recv.at[kind, chip], (row, other))
        pair.start()
        pending.append(pair)

    def share_line(kind, reach):
        part = slab.at[me, :, spans[kind]]
        for i in reach:
            there = mixed(chip, i, chips)
            line = remote(part, part, line_send.at[kind, there], line_recv.at[kind, chip], (row, there * 2 + core))
            line.start()
            pending.append(line)

    chip_group = share_group // 2
    mine = chip // chip_group
    all_chips = range(1, chips)

    def exchange(at, down_from, up_from, top, bottom, held):
        half = columns // 2
        left, right = pl.ds(0, half), pl.ds(half, half)
        send, recv = halo_send.at[at], halo_recv.at[at]

        def flow(index, source, target, cols, device):
            return remote(source.at[:, cols], target.at[:, cols], send.at[index], recv.at[index], device)

        above = [flow(0, down_from, top, left, (down, me)), flow(1, down_from, top, right, (down, me))]
        below = [flow(2, up_from, bottom, left, (up, me)), flow(3, up_from, bottom, right, (up, me))]
        starts = []
        relays = []
        if detour:
            starts.append((row == 1, remote(down_from.at[:, right], held, send.at[1], recv.at[4], (across, me))))
            starts.append((row == 2, remote(up_from.at[:, right], held, send.at[3], recv.at[4], (across, me))))
            relays.append((row == 3, remote(held, top.at[:, right], send.at[4], recv.at[1], (up, me))))
            relays.append((row == 0, remote(held, bottom.at[:, right], send.at[4], recv.at[3], (down, me))))
        starts.append((has_down & (row != 1) if detour else has_down, above[1]))
        starts.append((has_up & (row != 2) if detour else has_up, below[1]))
        parts = [[(has_down, above[0]), (has_up, below[0])], starts]

        def start(half):
            for here, copy in parts[half]:
                pl.when(here)(copy.start)

        def relay():
            for here, copy in relays:
                arrival = remote(held, held, send.at[4], recv.at[4], (across, me))

                @pl.when(here)
                def _():
                    arrival.wait_recv()
                    copy.start()

        def wait_recv(half):
            pl.when(has_up)(above[half].wait_recv)
            pl.when(has_down)(below[half].wait_recv)

        def wait_send():
            for here, copy in parts[0] + parts[1] + relays:
                pl.when(here)(copy.wait_send)

        return start, relay, wait_recv, wait_send

    early = exchange(
        0, x_ref.at[pl.ds(rows - HALO, HALO)], x_ref.at[pl.ds(0, HALO)],
        work.at[pl.ds(0, HALO)], work.at[pl.ds(HALO + rows, HALO)], relayed,
    )
    final = exchange(
        1, work.at[pl.ds(HALO + rows - BAND, BAND)], work.at[pl.ds(HALO, BAND)], ex.at[0], ex.at[1], late,
    )

    def forward(kind, reach):
        for i in reach:
            there = mixed(chip, i, chips)
            slot = slab.at[there * 2 + core, :, spans[kind]]
            copy = remote(slot, slot, pair_send.at[kind, there], pair_recv.at[kind, there], (row, other))
            remote(slot, slot, own_sem, line_recv.at[kind, there], (row, other)).wait_recv()
            copy.start()
            pending.append(copy)

    def landed(kind, reach):
        for i in reach:
            there = mixed(chip, i, chips)
            slot = slab.at[there * 2 + 1 - core, :, spans[kind]]
            remote(slot, slot, own_sem, pair_recv.at[kind, there], (row, other)).wait_recv()

    def taken(group, at):
        part = slab[pl.ds(group * share_group, share_group), :, pl.ds(at, WIN)]
        return part.reshape(BAND, WIN)

    def build(pairs):
        picks = []
        for sides in pairs:
            parts = [taken(group, order.index(tile) * WIN) for group, tile in sides]
            slots = [(group, 2 * tile + half) for half, (group, tile) in enumerate(sides)]
            picks.append((parts, slots))
        build_windows(own, rows_axis, picks, q_ref)

    tiles = len(order)
    others = [mixed(mine, i, GROUPS) for i in range(1, GROUPS)]
    inside, beyond = range(1, chip_group), range(chip_group, 2 * chip_group)
    near_by, far_off = range(1, 2 * chip_group), range(2 * chip_group, chips)
    share_pair(0)
    share_pair(2)
    share_line(0, near_by)
    share_line(2, near_by)
    share_line(0, far_off)
    early[0](1)
    early[0](0)
    for kind in (0, 2):
        forward(kind, inside)
    for kind in (0, 2):
        landed(kind, range(chip_group))
    build([((mine, tile),) * 2 for tile in range(tiles - 1)])
    pl.when(gets_near)(tail.wait_recv)
    slab[me, :, last:] = jnp.where(
        lax.broadcasted_iota(jnp.int32, edge.shape, 1) < BAND, edge[...], pltpu.roll(beside[...], BAND, 1)
    )
    share_pair(1)
    share_line(1, all_chips)
    early[1]()
    for kind in (0, 2):
        forward(kind, beyond)
    for kind in (0, 2):
        landed(kind, beyond)
    build([((others[0], tile),) * 2 for tile in range(tiles - 1)])
    share_line(2, far_off)
    forward(0, far_off)
    forward(1, all_chips)
    landed(0, far_off)
    landed(1, range(chips))
    ends = [(group, tile) for tile in (0, tiles - 2) for group in others[1:]]
    ends += [(group, tiles - 1) for group in range(GROUPS - 1)]
    build([(pair, pair) for pair in ends])

    def window(group, k):
        return group, k, HALO + BAND * (group % 2) + WIN * k, 0, WIN

    edges = [
        (0, own, 0, BAND, WIN),
        window(0, 0),
        window(0, 1),
        window(0, own - 2),
        window(0, own - 1),
        (2, own, HALO + rows, 0, BAND),
        (1, own, HALO - BAND, BAND, WIN),
        window(1, 0),
        window(1, own - 2),
        (1, own - 1, HALO + rows - BAND, 0, BAND),
        window(2, 0),
        window(2, own - 1),
    ]
    inner = [window(0, k) for k in range(2, own - 2)]
    inner += [window(1, k) for k in range(1, own - 2)]
    inner += [window(2, k) for k in range(1, own - 1)]

    fill.wait()
    forward(2, far_off)
    halves = [pl.ds(half * (columns // 2), columns // 2) for half in range(2)]
    for half in (0, 1):
        early[2](half)
        apply_windows(edges, q_ref, work, halves[half])
        final[0](half)
    landed(2, far_off)
    under = [(group, tile) for tile in range(1, tiles - 2) for group in others[1:]]
    build([(pair, pair) for pair in under + [(GROUPS - 1, tiles - 1)]])
    final[1]()
    for half in halves:
        apply_windows(inner, q_ref, work, half)

    def finish(cols):
        for k in range(own - 1):
            at = BAND + WIN * k
            out_ref[at : at + WIN, cols] = turn(q_ref[3, k], work[HALO + at : HALO + at + WIN, cols])

    for half in halves:
        finish(half)

    def straddle(cols):
        x = jnp.concatenate([ex[0, :, cols], work[HALO : HALO + BAND, cols]], 0)
        out_ref[:BAND, cols] = turn(q_ref[3, own, BAND:], x)
        x = jnp.concatenate([work[HALO + rows - BAND : HALO + rows, cols], ex[1, :, cols]], 0)
        out_ref[rows - BAND :, cols] = turn(q_ref[3, own - 1, :BAND], x)

    pl.when(sends_tail)(tail.wait_send)
    pl.when(sends_head)(head.wait_send)
    early[3]()
    for copy in pending:
        copy.wait_send()
    for half in (0, 1):
        final[2](half)
        straddle(halves[half])
    final[3]()


def shards(vectors, reflectors):
    rows, columns = vectors.shape
    own = rows // WIN
    rows_axis, cols_axis = lax.axis_size("row"), lax.axis_size("col")
    slots, stored = reflectors.shape
    chips = cols_axis // 2
    dma = pltpu.SemaphoreType.DMA
    return pl.pallas_call(
        functools.partial(back_kernel, own, rows_axis, cols_axis),
        in_specs=[pl.BlockSpec(memory_space=pltpu.HBM)] * 2,
        out_specs=pl.BlockSpec(memory_space=pltpu.VMEM),
        out_shape=jax.ShapeDtypeStruct(vectors.shape, vectors.dtype),
        scratch_shapes=[
            pltpu.VMEM((GROUPS, own + 1, WIN, 2 * WIN), jnp.bfloat16),
            pltpu.VMEM((rows + 2 * HALO, columns), jnp.float32),
            pltpu.VMEM((slots, stored), jnp.float32),
            pltpu.VMEM((slots, WIN), jnp.float32),
            pltpu.VMEM((slots, WIN), jnp.float32),
            pltpu.VMEM((cols_axis, slots, stored + BAND), jnp.float32),
            pltpu.VMEM((2, BAND, columns), jnp.float32),
            pltpu.VMEM((HALO, columns // 2), jnp.float32),
            pltpu.VMEM((BAND, columns // 2), jnp.float32),
            dma((2,)),
            dma((1,)),
            dma((3, chips)),
            dma((3, chips)),
            dma((3, chips)),
            dma((3, chips)),
            dma((2, 5)),
            dma((2, 5)),
            dma,
            dma,
        ],
        compiler_params=pltpu.CompilerParams(collective_id=0, has_side_effects=True, vmem_limit_bytes=50 * 2**20),
        name="back",
    )(reflectors, vectors)


def solution(mesh):
    placed = (P("row", "col"), P("col", "row"))
    return jax.shard_map(
        shards, mesh=mesh, in_specs=placed, out_specs=P("row", "col"), check_vma=False
    )
```

```python
import functools

import jax
import jax.numpy as jnp
from jax import lax
from jax.experimental import pallas as pl
from jax.experimental.pallas import tpu as pltpu
from jax.sharding import PartitionSpec as P

BAND = 64
GROUPS = 4
WIN = 2 * BAND
HALO = 2 * BAND


def split(x):
    high = x.astype(jnp.bfloat16)
    low = (x - high.astype(jnp.float32)).astype(jnp.bfloat16)
    return high, low


def dot(a, b, dims=(1, 0)):
    return lax.dot_general(
        a, b, (((dims[0],), (dims[1],)), ((), ())), preferred_element_type=jnp.float32
    )


def product(a, b):
    ah, al = split(a)
    bh, bl = split(b)
    return dot(jnp.concatenate([ah, al, ah], 1), jnp.concatenate([bh, bh, bl], 0))


def keep(q, q_ref, group, k):
    high, low = split(q)
    q_ref[group, k, :, :WIN] = high
    q_ref[group, k, :, WIN:] = low


def build_windows(own, rows_axis, picks, q_ref):
    grid_row = lax.axis_index("row")
    size = WIN
    row = lax.broadcasted_iota(jnp.int32, (size, size), 0)
    lane = lax.broadcasted_iota(jnp.int32, (size, size), 1)
    eye = row == lane
    identity = eye.astype(jnp.float32)
    upper = (row // BAND == lane // BAND) & (row < lane)
    inside = (row // BAND) == (lane // BAND)
    lead = inside & (lane % BAND == 0)

    skews, nils, invs, scaled = [], [], [], []
    for (left, right), _ in picks:
        both = jnp.concatenate([left, right], 0)
        both = jnp.where(lead, 1.0, jnp.where(inside, both, 0.0))
        skews.append(pltpu.roll(both, 0, 1, stride=1, stride_axis=0))
    for skew in skews:
        high, low = split(skew)
        gram = dot(
            jnp.concatenate([high, low, high], 1), jnp.concatenate([high, high, low], 1), (1, 1)
        )
        diag = 0.5 * jnp.sum(jnp.where(eye, gram, 0.0), axis=1, keepdims=True)
        scale = 1.0 / diag
        nils.append(jnp.where(upper, gram * scale, 0.0))
        scaled.append(skew * scale)
    block = BAND // 2
    near = row // block == lane // block
    powers = [jnp.where(near, n, 0.0) for n in nils]
    invs = [identity - p for p in powers]
    powers = [product(p, p) for p in powers]
    for level in range(3):
        stacked = [product(jnp.concatenate([i, p], 0), p) for i, p in zip(invs, powers)]
        invs = [i + s[:size] for i, s in zip(invs, stacked)]
        powers = [s[size:] for s in stacked]
    invs = [i + product(i, p) for i, p in zip(invs, powers)]
    for _ in range(1):
        wide = row // (2 * block) == lane // (2 * block)
        far = wide & (row // block != lane // block)
        cross = [product(jnp.where(far, n, 0.0), i) for n, i in zip(nils, invs)]
        invs = [i - product(i, c) for i, c in zip(invs, cross)]
        block *= 2
    solved = [product(i, s) for i, s in zip(invs, scaled)]
    for (_, slots), skew, wing in zip(picks, skews, solved):
        sh, sl = split(skew)
        th, tl = split(wing)
        for half, (group, k) in enumerate(slots):
            own_rows = slice(half * BAND, (half + 1) * BAND)
            left = jnp.concatenate([sh[own_rows], sl[own_rows], sh[own_rows]], 0)
            right = jnp.concatenate([th[own_rows], th[own_rows], tl[own_rows]], 0)
            change = dot(left, right, (0, 0))
            outer = jnp.where(group == 2, grid_row < rows_axis - 1, grid_row > 0)
            inner = grid_row * own + k < own * rows_axis - group % 2
            q = identity - jnp.where(jnp.where(k == own, outer, inner), change, 0.0)
            keep(q, q_ref, group, k)


def mixed(a, b, count):
    total, bit = 0, 1
    while bit < count:
        total = total + ((a // bit + b // bit) % 2) * bit
        bit *= 2
    return total


def turn(q, x):
    xh, xl = split(x)
    return dot(q, jnp.concatenate([xh, xh], 0)) + dot(q[:, :WIN], xl)


def apply_windows(windows, q_ref, work, cols):
    for group, k, at, low, high in windows:
        y = turn(q_ref[group, k, low:high], work[at : at + WIN, cols])
        work[at + low : at + high, cols] = y


def tile_order(own):
    tiles = (own + 1) // 2
    return [0, tiles - 2] + list(range(1, tiles - 2)) + [tiles - 1]


def back_kernel(
    own, rows_axis, cols_axis, refl_ref, x_ref, out_ref,
    q_ref, work, raw, edge, beside, slab, ex, relayed, late,
    near_send, near_recv, line_send, line_recv, pair_send, pair_recv, halo_send, halo_recv, own_sem, x_sem,
):
    row, me = lax.axis_index("row"), lax.axis_index("col")
    chips = cols_axis // 2
    chip, core = me // 2, me % 2
    up, down = (row + rows_axis - 1) % rows_axis, (row + 1) % rows_axis
    other = chip * 2 + 1 - core
    rows, columns = x_ref.shape
    stored = raw.shape[1]
    order = tile_order(own)
    share_group = cols_axis // GROUPS
    group_of = me // share_group
    two = 2 * share_group
    has_up, has_down = row > 0, row < rows_axis - 1
    mesh_ids = pl.DeviceIdType.MESH
    no = jnp.logical_not
    detour = rows_axis == 4
    across = (row + 2) % rows_axis

    def remote(source, target, send, recv, device):
        return pltpu.make_async_remote_copy(
            src_ref=source, dst_ref=target, send_sem=send, recv_sem=recv,
            device_id=device, device_id_type=mesh_ids,
        )

    local = pltpu.make_async_copy(refl_ref, raw, own_sem)
    local.start()
    fill = pltpu.make_async_copy(x_ref, work.at[pl.ds(HALO, rows)], x_sem)
    fill.start()
    first, third = group_of == 0, group_of == 2
    barrier = pltpu.get_barrier_semaphore()
    partners = [(row, mixed(chip, i, chips) * 2 + core) for i in range(1, chips)]
    partners += [(row, other), (up, me), (down, me)]
    if detour:
        partners.append((across, me))

    def greet(partner):
        pl.semaphore_signal(barrier, inc=1, device_id=partner, device_id_type=mesh_ids)

    for partner in partners:
        greet(partner)
    pl.when(first)(lambda: greet((up, (me + two) % cols_axis)))
    pl.when(third)(lambda: greet((down, (me + cols_axis - two) % cols_axis)))

    @pl.when(no(has_up))
    def _():
        work[0:HALO] = jnp.zeros((HALO, columns), jnp.float32)
        ex[0] = jnp.zeros((BAND, columns), jnp.float32)

    @pl.when(no(has_down))
    def _():
        work[HALO + rows :] = jnp.zeros((HALO, columns), jnp.float32)
        ex[1] = jnp.zeros((BAND, columns), jnp.float32)

    gets_near = jnp.where(third, has_down, has_up)

    @pl.when(no(gets_near))
    def _():
        beside[...] = jnp.zeros(beside.shape, jnp.float32)

    local.wait()
    edge[:, :BAND] = raw[:, stored - BAND :]
    edge[:, BAND:] = jnp.zeros((raw.shape[0], BAND), jnp.float32)
    for at, tile in enumerate(order[:-1]):
        slab[me, :, at * WIN : (at + 1) * WIN] = raw[:, tile * WIN : (tile + 1) * WIN]
    pl.semaphore_wait(barrier, len(partners) + jnp.where(first | third, 1, 0))

    last = (len(order) - 1) * WIN
    spans = (pl.ds(0, 2 * WIN), pl.ds(last, WIN), pl.ds(2 * WIN, last - 2 * WIN))
    tail = remote(edge, beside, near_send.at[0], near_recv.at[0], (down, me))
    head = remote(slab.at[me, :, pl.ds(0, WIN)], beside, near_send.at[1], near_recv.at[0], (up, (me + two) % cols_axis))
    sends_tail = has_down & no(third)
    sends_head = has_up & first
    pl.when(sends_tail)(tail.start)
    pl.when(sends_head)(head.start)
    pending = []

    def share_pair(kind):
        part = slab.at[me, :, spans[kind]]
        pair = remote(part, part, pair_send.at[kind, chip], pair_recv.at[kind, chip], (row, other))
        pair.start()
        pending.append(pair)

    def share_line(kind, reach):
        part = slab.at[me, :, spans[kind]]
        for i in reach:
            there = mixed(chip, i, chips)
            line = remote(part, part, line_send.at[kind, there], line_recv.at[kind, chip], (row, there * 2 + core))
            line.start()
            pending.append(line)

    chip_group = share_group // 2
    mine = chip // chip_group
    all_chips = range(1, chips)

    def exchange(at, down_from, up_from, top, bottom, held):
        half = columns // 2
        left, right = pl.ds(0, half), pl.ds(half, half)
        send, recv = halo_send.at[at], halo_recv.at[at]

        def flow(index, source, target, cols, device):
            return remote(source.at[:, cols], target.at[:, cols], send.at[index], recv.at[index], device)

        above = [flow(0, down_from, top, left, (down, me)), flow(1, down_from, top, right, (down, me))]
        below = [flow(2, up_from, bottom, left, (up, me)), flow(3, up_from, bottom, right, (up, me))]
        starts = []
        relays = []
        if detour:
            starts.append((row == 1, remote(down_from.at[:, right], held, send.at[1], recv.at[4], (across, me))))
            starts.append((row == 2, remote(up_from.at[:, right], held, send.at[3], recv.at[4], (across, me))))
            relays.append((row == 3, remote(held, top.at[:, right], send.at[4], recv.at[1], (up, me))))
            relays.append((row == 0, remote(held, bottom.at[:, right], send.at[4], recv.at[3], (down, me))))
        starts.append((has_down & (row != 1) if detour else has_down, above[1]))
        starts.append((has_up & (row != 2) if detour else has_up, below[1]))
        parts = [[(has_down, above[0]), (has_up, below[0])], starts]

        def start(half):
            for here, copy in parts[half]:
                pl.when(here)(copy.start)

        def relay():
            for here, copy in relays:
                arrival = remote(held, held, send.at[4], recv.at[4], (across, me))

                @pl.when(here)
                def _():
                    arrival.wait_recv()
                    copy.start()

        def wait_recv(half):
            pl.when(has_up)(above[half].wait_recv)
            pl.when(has_down)(below[half].wait_recv)

        def wait_send():
            for here, copy in parts[0] + parts[1] + relays:
                pl.when(here)(copy.wait_send)

        return start, relay, wait_recv, wait_send

    early = exchange(
        0, x_ref.at[pl.ds(rows - HALO, HALO)], x_ref.at[pl.ds(0, HALO)],
        work.at[pl.ds(0, HALO)], work.at[pl.ds(HALO + rows, HALO)], relayed,
    )
    final = exchange(
        1, work.at[pl.ds(HALO + rows - BAND, BAND)], work.at[pl.ds(HALO, BAND)], ex.at[0], ex.at[1], late,
    )

    def forward(kind, reach):
        for i in reach:
            there = mixed(chip, i, chips)
            slot = slab.at[there * 2 + core, :, spans[kind]]
            copy = remote(slot, slot, pair_send.at[kind, there], pair_recv.at[kind, there], (row, other))
            remote(slot, slot, own_sem, line_recv.at[kind, there], (row, other)).wait_recv()
            copy.start()
            pending.append(copy)

    def landed(kind, reach):
        for i in reach:
            there = mixed(chip, i, chips)
            slot = slab.at[there * 2 + 1 - core, :, spans[kind]]
            remote(slot, slot, own_sem, pair_recv.at[kind, there], (row, other)).wait_recv()

    def taken(group, at):
        part = slab[pl.ds(group * share_group, share_group), :, pl.ds(at, WIN)]
        return part.reshape(BAND, WIN)

    def build(pairs):
        picks = []
        for sides in pairs:
            parts = [taken(group, order.index(tile) * WIN) for group, tile in sides]
            slots = [(group, 2 * tile + half) for half, (group, tile) in enumerate(sides)]
            picks.append((parts, slots))
        build_windows(own, rows_axis, picks, q_ref)

    tiles = len(order)
    others = [mixed(mine, i, GROUPS) for i in range(1, GROUPS)]
    inside, beyond = range(1, chip_group), range(chip_group, 2 * chip_group)
    near_by, far_off = range(1, 2 * chip_group), range(2 * chip_group, chips)
    share_pair(0)
    share_pair(2)
    share_line(0, near_by)
    share_line(2, near_by)
    share_line(0, far_off)
    early[0](1)
    early[0](0)
    for kind in (0, 2):
        forward(kind, inside)
    for kind in (0, 2):
        landed(kind, range(chip_group))
    build([((mine, tile),) * 2 for tile in range(tiles - 1)])
    pl.when(gets_near)(tail.wait_recv)
    slab[me, :, last:] = jnp.where(
        lax.broadcasted_iota(jnp.int32, edge.shape, 1) < BAND, edge[...], pltpu.roll(beside[...], BAND, 1)
    )
    share_pair(1)
    share_line(1, all_chips)
    early[1]()
    for kind in (0, 2):
        forward(kind, beyond)
    for kind in (0, 2):
        landed(kind, beyond)
    build([((others[0], tile),) * 2 for tile in range(tiles - 1)])
    share_line(2, far_off)
    forward(0, far_off)
    forward(1, all_chips)
    landed(0, far_off)
    landed(1, range(chips))
    ends = [(group, tile) for tile in (0, tiles - 2) for group in others[1:]]
    ends += [(group, tiles - 1) for group in range(GROUPS - 1)]
    build([(pair, pair) for pair in ends])

    def window(group, k):
        return group, k, HALO + BAND * (group % 2) + WIN * k, 0, WIN

    edges = [
        (0, own, 0, BAND, WIN),
        window(0, 0),
        window(0, 1),
        window(0, own - 2),
        window(0, own - 1),
        (2, own, HALO + rows, 0, BAND),
        (1, own, HALO - BAND, BAND, WIN),
        window(1, 0),
        window(1, own - 2),
        (1, own - 1, HALO + rows - BAND, 0, BAND),
        window(2, 0),
        window(2, own - 1),
    ]
    inner = [window(0, k) for k in range(2, own - 2)]
    inner += [window(1, k) for k in range(1, own - 2)]
    inner += [window(2, k) for k in range(1, own - 1)]

    fill.wait()
    forward(2, far_off)
    halves = [pl.ds(half * (columns // 2), columns // 2) for half in range(2)]
    for half in (0, 1):
        early[2](half)
        apply_windows(edges, q_ref, work, halves[half])
        final[0](half)
    landed(2, far_off)
    under = [(group, tile) for tile in range(1, tiles - 2) for group in others[1:]]
    build([(pair, pair) for pair in under + [(GROUPS - 1, tiles - 1)]])
    final[1]()
    for half in halves:
        apply_windows(inner, q_ref, work, half)

    def finish(cols):
        for k in range(own - 1):
            at = BAND + WIN * k
            out_ref[at : at + WIN, cols] = turn(q_ref[3, k], work[HALO + at : HALO + at + WIN, cols])

    for half in halves:
        finish(half)

    def straddle(cols):
        x = jnp.concatenate([ex[0, :, cols], work[HALO : HALO + BAND, cols]], 0)
        out_ref[:BAND, cols] = turn(q_ref[3, own, BAND:], x)
        x = jnp.concatenate([work[HALO + rows - BAND : HALO + rows, cols], ex[1, :, cols]], 0)
        out_ref[rows - BAND :, cols] = turn(q_ref[3, own - 1, :BAND], x)

    pl.when(sends_tail)(tail.wait_send)
    pl.when(sends_head)(head.wait_send)
    early[3]()
    for copy in pending:
        copy.wait_send()
    for half in (0, 1):
        final[2](half)
        straddle(halves[half])
    final[3]()


def shards(vectors, reflectors):
    rows, columns = vectors.shape
    own = rows // WIN
    rows_axis, cols_axis = lax.axis_size("row"), lax.axis_size("col")
    slots, stored = reflectors.shape
    chips = cols_axis // 2
    dma = pltpu.SemaphoreType.DMA
    return pl.pallas_call(
        functools.partial(back_kernel, own, rows_axis, cols_axis),
        in_specs=[pl.BlockSpec(memory_space=pltpu.HBM)] * 2,
        out_specs=pl.BlockSpec(memory_space=pltpu.VMEM),
        out_shape=jax.ShapeDtypeStruct(vectors.shape, vectors.dtype),
        scratch_shapes=[
            pltpu.VMEM((GROUPS, own + 1, WIN, 2 * WIN), jnp.bfloat16),
            pltpu.VMEM((rows + 2 * HALO, columns), jnp.float32),
            pltpu.VMEM((slots, stored), jnp.float32),
            pltpu.VMEM((slots, WIN), jnp.float32),
            pltpu.VMEM((slots, WIN), jnp.float32),
            pltpu.VMEM((cols_axis, slots, stored + BAND), jnp.float32),
            pltpu.VMEM((2, BAND, columns), jnp.float32),
            pltpu.VMEM((HALO, columns // 2), jnp.float32),
            pltpu.VMEM((BAND, columns // 2), jnp.float32),
            dma((2,)),
            dma((1,)),
            dma((3, chips)),
            dma((3, chips)),
            dma((3, chips)),
            dma((3, chips)),
            dma((2, 5)),
            dma((2, 5)),
            dma,
            dma,
        ],
        compiler_params=pltpu.CompilerParams(collective_id=0, has_side_effects=True, vmem_limit_bytes=50 * 2**20),
        name="back",
    )(reflectors, vectors)


def solution(mesh):
    placed = (P("row", "col"), P("col", "row"))
    return jax.shard_map(
        shards, mesh=mesh, in_specs=placed, out_specs=P("row", "col"), check_vma=False
    )
```
